32 devices in a mesh: lat: 4 (over y, x), kpt: 8 (over z, core).
Axes of the slice: x: 2, y: 2, z: 4, core: 2. Of those that a mesh axis runs over, the one named last changes fastest.
Arguments:
- coarse: bfloat16 [2, 4, 32, 12288], P(None, 'lat', 'kpt'), may hold values from -1 to 1
- rp_vectors: int32 [4, 3], P('lat'), may hold values from -4 to 4
- rp_weights: int32 [4], P('lat'), may hold values from 1 to 3
- re_vectors: int32 [32, 3], replicated, may hold values from -4 to 4
- re_weights: int32 [32], replicated, may hold values from 1 to 3
- q_points: float32 [2, 3], replicated, may hold values from 0 to 1
- k_points: float32 [512, 3], P('kpt'), may hold values from 0 to 1
- modes_rot: bfloat16 [2, 2, 48, 48], replicated, may hold values from -0.625 to 0.625
- u_k: bfloat16 [2, 512, 16, 16], P(None, 'kpt'), may hold values from -1 to 1
- u_kq: bfloat16 [2, 2, 512, 16, 16], P(None, None, 'kpt'), may hold values from -1 to 1
- mask_k: int32 [512, 16], P('kpt'), may hold values 0 or 1
- mask_kq: int32 [2, 512, 16], P(None, 'kpt'), may hold values 0 or 1
Outputs:
- coupling: bfloat16 [2, 512, 2, 12288], P(None, 'kpt', None, 'lat')
The draws below stay inside these ranges and needn't reach their ends.
All inputs are finite; a program needn't handle non-finite values. No bound on the sum of `mask_k` or of `mask_kq` on one device may be relied on, other than what follows from the above.
Results may differ from the reference program's by a relative error of at most 0.017.
Values may be sent and summed in bfloat16 or wider, within the bound.
A program may use at most 128 MiB of HBM per device.

```python
import jax
import jax.numpy as jnp
from jax import lax

W = 16
M = 48
NQ = 2
NK = 512
NRP = 4
NRE = 32


def touch_ends(entries, stream_key, least, largest):
    index_at = [jax.random.randint(jax.random.fold_in(stream_key, axis), (), 0, length) for axis, length in enumerate(entries.shape)]
    longest = entries.shape.index(max(entries.shape))
    neighbour = index_at[:longest] + [(index_at[longest] + 1) % entries.shape[longest]] + index_at[longest + 1:]
    return entries.at[tuple(index_at)].set(least).at[tuple(neighbour)].set(largest)


def steps_of(key, extent, cuts, least, top_value):
    def one(dim, shards_of):
        steps = jax.random.uniform(jax.random.fold_in(jax.random.fold_in(key, 6), dim), (shards_of,), jnp.float32, least / len(cuts), top_value / len(cuts))
        return jnp.repeat(jnp.exp(steps), extent[dim] // shards_of).reshape((-1,) + (1,) * (len(extent) - dim - 1))

    gain = one(*cuts[0])
    for cut in cuts[1:]:
        gain = gain * one(*cut)
    return gain


def scatter_about(stream_key, shape, scale, reach, split=(), dtype=jnp.bfloat16):
    drawn = jax.random.normal(stream_key, shape, jnp.float32) * scale
    if len(split) > 0:
        drawn = steps_of(stream_key, shape, split, -0.22, 0.18) * drawn
    return jnp.clip(drawn, min=-reach, max=reach).astype(dtype)


def setup_inputs(seed: int = 0) -> dict:
    arg_keys = jax.random.split(jax.random.key(seed), 13)
    return {
        "coarse": scatter_about(arg_keys[0], (2, NRP, NRE, M * W * W), (NRP * NRE // 4) ** -0.5, 1.0, ((1, 4), (2, 8))),
        "rp_vectors": touch_ends(jax.random.randint(arg_keys[1], (NRP, 3), -4, 5), jax.random.fold_in(arg_keys[1], 1), -4, 4).astype(jnp.int32),
        "rp_weights": touch_ends(jax.random.randint(arg_keys[2], (NRP,), 1, 4), jax.random.fold_in(arg_keys[2], 1), 1, 3).astype(jnp.int32),
        "re_vectors": touch_ends(jax.random.randint(arg_keys[3], (NRE, 3), -4, 5), jax.random.fold_in(arg_keys[3], 1), -4, 4).astype(jnp.int32),
        "re_weights": touch_ends(jax.random.randint(arg_keys[4], (NRE,), 1, 4), jax.random.fold_in(arg_keys[4], 1), 1, 3).astype(jnp.int32),
        "q_points": jnp.clip(jax.random.uniform(arg_keys[5], (NQ, 3), jnp.float32, 0.0, 1.0), 0.0, 1.0),
        "k_points": jnp.clip(1.0 * jax.random.uniform(arg_keys[6], (NK, 3), jnp.float32) ** steps_of(arg_keys[6], (NK, 3), ((0, 8),), -0.2, 0.2), 0.0, 1.0),
        "modes_rot": scatter_about(arg_keys[7], (2, NQ, M, M), (2 * M) ** -0.5, 0.625),
        "u_k": scatter_about(arg_keys[8], (2, NK, W, W), (2 * W) ** -0.5, 1.0, ((1, 8),)),
        "u_kq": scatter_about(arg_keys[9], (2, NQ, NK, W, W), (2 * W) ** -0.5, 1.0, ((2, 8),)),
        "mask_k": touch_ends((jax.random.randint(arg_keys[10], (NK, W), 0, 4) < 3).astype(jnp.int32), jax.random.fold_in(arg_keys[10], 1), 0, 1),
        "mask_kq": touch_ends((jax.random.randint(arg_keys[11], (NQ, NK, W), 0, 4) < 3).astype(jnp.int32), jax.random.fold_in(arg_keys[11], 1), 0, 1),
    }


two_pi = 6.283185307179586


def phases(points, vectors, weights):
    cells = vectors.astype(jnp.float32)
    argument = two_pi * (points[:, 0:1] * cells[None, :, 0] + points[:, 1:2] * cells[None, :, 1] + points[:, 2:3] * cells[None, :, 2])
    inverse = 1.0 / weights.astype(jnp.float32)
    return (jnp.cos(argument) * inverse).astype(jnp.bfloat16), (jnp.sin(argument) * inverse).astype(jnp.bfloat16)


def reference(coarse, rp_vectors, rp_weights, re_vectors, re_weights, q_points, k_points, modes_rot, u_k, u_kq, mask_k, mask_kq):
    high = lax.Precision.HIGHEST
    phase_real, phase_imag = phases(q_points, rp_vectors, rp_weights)
    flat_real = coarse[0].reshape(NRP, NRE * M * W * W)
    flat_imag = coarse[1].reshape(NRP, NRE * M * W * W)
    part_real = jnp.dot(phase_real, flat_real, preferred_element_type=jnp.float32) - jnp.dot(phase_imag, flat_imag, preferred_element_type=jnp.float32)
    part_imag = jnp.dot(phase_real, flat_imag, preferred_element_type=jnp.float32) + jnp.dot(phase_imag, flat_real, preferred_element_type=jnp.float32)
    on_q = jnp.stack([part_real, part_imag]).astype(jnp.bfloat16)
    values = lax.optimization_barrier(on_q).astype(jnp.float32).reshape(2, NQ, NRE, M, W * W)
    eigen = modes_rot.astype(jnp.float32)
    br = jnp.einsum("qmn,qrmx->qrnx", eigen[0], values[0], precision=high) - jnp.einsum("qmn,qrmx->qrnx", eigen[1], values[1], precision=high)
    bi = jnp.einsum("qmn,qrmx->qrnx", eigen[0], values[1], precision=high) + jnp.einsum("qmn,qrmx->qrnx", eigen[1], values[0], precision=high)
    branch = jnp.stack([br, bi]).reshape(2, NQ, NRE, M * W * W).astype(jnp.bfloat16)
    kreal, kimag = phases(k_points, re_vectors, re_weights)
    kreal = kreal.astype(jnp.float32)
    kimag = kimag.astype(jnp.float32)
    grid = lax.optimization_barrier(branch).astype(jnp.float32)
    er = jnp.einsum("kr,qrx->kqx", kreal, grid[0], precision=high) - jnp.einsum("kr,qrx->kqx", kimag, grid[1], precision=high)
    ei = jnp.einsum("kr,qrx->kqx", kreal, grid[1], precision=high) + jnp.einsum("kr,qrx->kqx", kimag, grid[0], precision=high)
    bloch = jnp.stack([er, ei]).astype(jnp.bfloat16)
    field = lax.optimization_barrier(bloch).astype(jnp.float32).reshape(2, NK, NQ, M, W, W)
    right = u_k.astype(jnp.float32)
    left = u_kq.astype(jnp.float32)
    tr = jnp.einsum("kqmab,kbn->kqman", field[0], right[0], precision=high) - jnp.einsum("kqmab,kbn->kqman", field[1], right[1], precision=high)
    ti = jnp.einsum("kqmab,kbn->kqman", field[0], right[1], precision=high) + jnp.einsum("kqmab,kbn->kqman", field[1], right[0], precision=high)
    half = lax.optimization_barrier(jnp.stack([tr, ti]).astype(jnp.bfloat16)).astype(jnp.float32)
    tr = half[0]
    ti = half[1]
    outr = jnp.einsum("qkac,kqman->kqmcn", left[0], tr, precision=high) + jnp.einsum("qkac,kqman->kqmcn", left[1], ti, precision=high)
    outi = jnp.einsum("qkac,kqman->kqmcn", left[0], ti, precision=high) - jnp.einsum("qkac,kqman->kqmcn", left[1], tr, precision=high)
    window = jnp.transpose(mask_kq.astype(jnp.float32), (1, 0, 2))[:, :, None, :, None] * mask_k.astype(jnp.float32)[:, None, None, None, :]
    result = jnp.stack([outr * window, outi * window])
    return result.reshape(2, NK, NQ, M * W * W).astype(jnp.bfloat16)
```

```python
import functools

import jax
import jax.numpy as jnp
from jax import lax
from jax.experimental import pallas as pl
from jax.experimental.pallas import tpu as pltpu
from jax.sharding import PartitionSpec as P

two_pi = 6.283185307179586
f32 = jnp.float32
bf16 = jnp.bfloat16
i32 = jnp.int32
MESH = pl.DeviceIdType.MESH
LANES = 128


def up(value, step):
    return -(-value // step) * step


def iota(shape, axis):
    return lax.broadcasted_iota(i32, shape, axis)


def dot(a, b):
    return jnp.dot(a, b, preferred_element_type=f32)


def exchange(tiles, unit):
    span = LANES // unit
    shape = next(t for t in tiles if t is not None).shape
    lane = iota(shape, 1)
    bit = 1
    while bit < span:
        shift = unit * bit
        odd = (lane & shift) != 0
        turned = list(tiles)
        for i in range(span):
            if i & bit:
                continue
            a, b = tiles[i], tiles[i | bit]
            if a is None:
                continue
            ahead = pltpu.roll(a, LANES - shift, 1)
            if b is None:
                turned[i], turned[i | bit] = a, ahead
            else:
                turned[i] = jnp.where(odd, pltpu.roll(b, shift, 1), a)
                turned[i | bit] = jnp.where(odd, b, ahead)
        tiles = turned
        bit *= 2
    return tiles


def kernel(
    lat_count,
    kpt_count,
    modes,
    rpv,
    rpw,
    qp,
    x_ref,
    rot_ref,
    rv_ref,
    rw_ref,
    kp_ref,
    u_ref,
    v_ref,
    mk_ref,
    mkq_ref,
    out_ref,
    xs,
    wre,
    wim,
    part,
    recv,
    turned,
    gath,
    p2,
    u2,
    gs,
    vb,
    rt,
    lat_send,
    lat_recv,
    chip_send,
    chip_recv,
    pair_send,
    pair_recv,
):
    lat = lax.axis_index("lat")
    kpt = lax.axis_index("kpt")
    chips = kpt_count // 2
    chip = kpt // 2
    core = kpt - 2 * chip
    pair = 2 * chip + 1 - core

    def lat_peer(step):
        return lax.rem(lat + step, lat_count)

    def chip_peer(step):
        return lax.rem(chip + step, chips)

    barrier = pltpu.get_barrier_semaphore()
    for step in range(1, lat_count):
        pl.semaphore_signal(barrier, inc=1, device_id=(lat_peer(step), kpt), device_id_type=MESH)
    for step in range(1, chips):
        pl.semaphore_signal(barrier, inc=1, device_id=(lat, 2 * chip_peer(step) + core), device_id_type=MESH)
    pl.semaphore_signal(barrier, inc=1, device_id=(lat, pair), device_id_type=MESH)

    q_count = rot_ref.shape[1]
    mode_count = rot_ref.shape[2]
    local = x_ref.shape[2]
    bands = mk_ref.shape[0]
    k_count = mk_ref.shape[1]
    width = bands * bands
    halves = width // LANES
    cells = rv_ref.shape[1]
    qn = part.shape[2] // 2
    span = LANES // bands

    if q_count * modes != qn:
        wre[...] = jnp.zeros_like(wre)
        wim[...] = jnp.zeros_like(wim)
    for q in range(q_count):
        argument = two_pi * (
            qp[q, 0] * rpv[0, 0].astype(f32)
            + qp[q, 1] * rpv[0, 1].astype(f32)
            + qp[q, 2] * rpv[0, 2].astype(f32)
        )
        argument = jnp.full((8, LANES), argument, f32)
        inverse = 1.0 / jnp.full((8, LANES), rpw[0].astype(f32), f32)
        pr = (jnp.cos(argument) * inverse).astype(bf16).astype(f32)[:1, :mode_count]
        pi = (jnp.sin(argument) * inverse).astype(bf16).astype(f32)[:1, :mode_count]
        mr = rot_ref[0, q].astype(f32).T
        mi = rot_ref[1, q].astype(f32).T
        wr = pr * mr - pi * mi
        wi = pr * mi + pi * mr
        for d in range(lat_count):
            rows = slice(d * modes, (d + 1) * modes)
            at = d * 2 * qn + q * modes
            wre[at : at + modes, :] = wr[rows]
            wim[at : at + modes, :] = -wi[rows]
            wre[at + qn : at + qn + modes, :] = wi[rows]
            wim[at + qn : at + qn + modes, :] = wr[rows]

    for c in range(2):
        x = x_ref[c, 0].astype(f32)
        for m in range(mode_count):
            for h in range(halves):
                at = (h * mode_count + m) * 2 * local + c * local
                lane = m * width + h * LANES
                xs[at : at + local, :] = x[:, lane : lane + LANES]

    def rows_of(c, e):
        return jnp.concatenate(
            [
                xs[pl.ds(h * mode_count * 2 * local + c * local + e, mode_count, stride=2 * local), :]
                for h in range(halves)
            ],
            axis=1,
        ).astype(bf16)

    left, right = wre[...].astype(bf16), wim[...].astype(bf16)
    for e in range(local):
        piece = (dot(left, rows_of(0, e)) + dot(right, rows_of(1, e))).astype(bf16)
        for d in range(lat_count):
            part[d, e] = piece[d * 2 * qn : (d + 1) * 2 * qn]

    pl.semaphore_wait(barrier, lat_count + chips - 1)
    first = []
    for step in range(1, lat_count):
        copy = pltpu.make_async_remote_copy(
            src_ref=part.at[lat_peer(step)],
            dst_ref=recv.at[lat],
            send_sem=lat_send.at[step],
            recv_sem=lat_recv.at[step],
            device_id=(lat_peer(step), kpt),
            device_id_type=MESH,
        )
        copy.start()
        first.append(copy)

    size = bands * k_count
    spread = iota((k_count, size), 1) - bands * iota((k_count, size), 0)
    spread = ((spread >= 0) & (spread < bands)).astype(f32).astype(bf16)
    eye = iota((cells, cells), 0) == iota((cells, cells), 1)

    def column(row):
        return jnp.sum(jnp.where(eye, row, 0.0), axis=1, keepdims=True)

    column_of = [column(rv_ref[i : i + 1, :].astype(f32)) for i in range(3)]
    argument = two_pi * (
        kp_ref[0:1, :] * column_of[0] + kp_ref[1:2, :] * column_of[1] + kp_ref[2:3, :] * column_of[2]
    )
    inverse = 1.0 / column(rw_ref[...].astype(f32))
    p2[0] = dot((jnp.cos(argument) * inverse).astype(bf16), spread)
    p2[1] = dot((jnp.sin(argument) * inverse).astype(bf16), spread)

    row = iota((width, size), 0)
    lane = iota((width, size), 1) & (bands - 1)
    pick = iota((bands, width), 1)
    order = iota((bands, width), 0)
    minor = (row & (bands - 1)) == lane
    major = (row // bands) == lane
    take_major = ((pick // bands) == order).astype(f32).astype(bf16)
    take_minor = ((pick & (bands - 1)) == order).astype(f32).astype(bf16)
    keep = jnp.concatenate([mk_ref[...].astype(f32)] * bands, axis=0)
    for c in range(2):
        wide = dot((u_ref[c].astype(f32) * keep).astype(bf16), spread)
        u2[c] = dot(take_major, jnp.where(minor, wide, 0.0).astype(bf16))
    blocks = gs.shape[0] // 2
    lanes = gs.shape[2]

    def grow(e, carry):
        pr, pi = p2[0, pl.ds(e, 1), :], p2[1, pl.ds(e, 1), :]
        re = (pr * u2[0] - pi * u2[1]).astype(bf16)
        im = pr * u2[1] + pi * u2[0]
        minus = (-im).astype(bf16)
        im = im.astype(bf16)
        at = pl.ds(pl.multiple_of(e * 2 * bands, bands), bands)
        below = pl.ds(pl.multiple_of(e * 2 * bands + bands, bands), bands)
        for t in range(blocks):
            cut = slice(t * lanes, (t + 1) * lanes)
            gs[t, at, :] = re[:, cut]
            gs[blocks + t, at, :] = im[:, cut]
            gs[t, below, :] = minus[:, cut]
            gs[blocks + t, below, :] = re[:, cut]
        return carry

    lax.fori_loop(0, cells, grow, 0)

    turn = []
    for q in range(q_count):
        keep = jnp.concatenate([mkq_ref[q].astype(f32)] * bands, axis=0)
        for c in range(2):
            wide = dot((v_ref[c, q].astype(f32) * keep).astype(bf16), spread)
            turn.append(dot(take_minor, jnp.where(major, wide, 0.0).astype(bf16)))
    tall = 2 * bands * span * q_count
    row = iota((tall, LANES), 0)
    place = row & (span * q_count - 1)
    same = [
        (place // q_count == iota((tall, LANES), 1) // bands) & (place % q_count == q) for q in range(q_count)
    ]
    repeat = (iota((tall, 2 * bands), 0) // (span * q_count)) == iota((tall, 2 * bands), 1)
    repeat = repeat.astype(f32).astype(bf16)
    for o in range(k_count // span):
        cut = slice(o * LANES, (o + 1) * LANES)
        for q in range(q_count):
            re, im = turn[2 * q][:, cut], turn[2 * q + 1][:, cut]
            both = [jnp.concatenate([re, -im], axis=0), jnp.concatenate([im, re], axis=0)]
            for c in range(2):
                wide = jnp.where(same[q], dot(repeat, both[c].astype(bf16)), 0.0)
                at = (q * 2 + c) * LANES
                vb[o, :, at : at + LANES] = wide.astype(bf16)

    for copy in first:
        copy.wait_recv()
    cut = span // 2
    for g in range(local // cut):
        rows = []
        for e in range(g * cut, (g + 1) * cut):
            total = part[lat, e].astype(f32)
            for step in range(1, lat_count):
                total = total + recv[lat_peer(step), e].astype(f32)
            rows += [total[:qn], total[qn:]]
        for h in range(halves):
            tiles = exchange([r[:, h * LANES : (h + 1) * LANES] for r in rows], bands)
            for a in range(span):
                turned[pl.ds(h * span + a, qn, stride=bands), :] = tiles[a]
        gath[kpt, g] = turned[...].astype(bf16)

    second = []
    for step in range(1, chips):
        copy = pltpu.make_async_remote_copy(
            src_ref=gath.at[kpt],
            dst_ref=gath.at[kpt],
            send_sem=chip_send.at[step],
            recv_sem=chip_recv.at[step],
            device_id=(lat, 2 * chip_peer(step) + core),
            device_id_type=MESH,
        )
        copy.start()
        second.append(copy)
    third = []
    for step in range(chips):
        source = 2 * lax.rem(chip + chips - step, chips) + core
        if step > 0:
            second[step - 1].wait_recv()
        copy = pltpu.make_async_remote_copy(
            src_ref=gath.at[source],
            dst_ref=gath.at[source],
            send_sem=pair_send.at[step],
            recv_sem=pair_recv.at[step],
            device_id=(lat, pair),
            device_id_type=MESH,
        )
        copy.start()
        third.append(copy)
    for copy in third:
        copy.wait_recv()

    groups = local // cut
    octets = -(-modes // span)
    near = lanes // LANES
    full = jnp.concatenate([gath[j, g] for j in range(kpt_count) for g in range(groups)], axis=1)

    def finish(t, carry):
        field = [dot(full, gs[c * blocks + t]) for c in range(2)]
        for o in range(near):
            for q in range(q_count):
                for c in range(2):
                    for s in range(octets):
                        tiles = []
                        for i in range(span):
                            m = s * span + i
                            at = (q * modes + m) * bands
                            tiles.append(
                                field[c][at : at + bands, o * LANES : (o + 1) * LANES] if m < modes else None
                            )
                        tiles = exchange(tiles, bands)
                        for i in range(span):
                            at = ((q * 2 + c) * span + i) * bands
                            rt[o, at : at + bands, s * LANES : (s + 1) * LANES] = tiles[i].astype(bf16)
            done = dot(vb[t * near + o], rt[o])
            rows = span * q_count
            for c in range(2):
                for h in range(bands // span):
                    for s in range(octets):
                        tiles = []
                        for i in range(span):
                            at = (c * bands + h * span + i) * rows
                            tiles.append(done[at : at + rows, s * LANES : (s + 1) * LANES])
                        tiles = exchange(tiles, bands)
                        for i in range(min(span, modes - s * span)):
                            at = (s * span + i) * width + h * LANES
                            k = pl.ds(pl.multiple_of((t * near + o) * span, span), span)
                            out_ref[c, k, :, at : at + LANES] = (
                                tiles[i].astype(bf16).reshape(span, q_count, LANES)
                            )
        return carry

    lax.fori_loop(0, blocks, finish, 0)
    for copy in first + second + third:
        copy.wait_send()


def per_device(
    lat_count,
    kpt_count,
    coarse,
    rp_vectors,
    rp_weights,
    re_vectors,
    re_weights,
    q_points,
    k_points,
    modes_rot,
    u_k,
    u_kq,
    mask_k,
    mask_kq,
):
    q_count = q_points.shape[0]
    k_count = k_points.shape[0]
    bands = u_k.shape[2]
    width = bands * bands
    local = coarse.shape[2]
    mode_count = coarse.shape[3] // width
    modes = mode_count // lat_count
    cells = re_vectors.shape[0]
    span = LANES // bands
    qn = up(q_count * modes, 8)
    groups = local // (span // 2)
    octets = -(-modes // span)
    chips = kpt_count // 2
    lanes = 2 * LANES
    blocks = bands * k_count // lanes
    assert coarse.shape[1] == 1 and local % (span // 2) == 0 and bands & (bands - 1) == 0

    uk = jnp.transpose(u_k, (0, 2, 3, 1)).reshape(2, width, k_count)
    ukq = jnp.transpose(u_kq, (0, 1, 3, 4, 2)).reshape(2, q_count, width, k_count)
    keep_k = jnp.transpose(mask_k)
    keep_kq = jnp.transpose(mask_kq, (0, 2, 1))

    smem = pl.BlockSpec(memory_space=pltpu.SMEM)
    vmem = pl.BlockSpec(memory_space=pltpu.VMEM)
    dma = pltpu.SemaphoreType.DMA
    tall = span * q_count * 2 * bands
    return pl.pallas_call(
        functools.partial(kernel, lat_count, kpt_count, modes),
        in_specs=[smem] * 3 + [vmem] * 9,
        out_specs=vmem,
        out_shape=jax.ShapeDtypeStruct((2, k_count, q_count, modes * width), bf16),
        scratch_shapes=[
            pltpu.VMEM((2 * local * mode_count * (width // LANES), LANES), f32),
            pltpu.VMEM((lat_count * 2 * qn, mode_count), f32),
            pltpu.VMEM((lat_count * 2 * qn, mode_count), f32),
            pltpu.VMEM((lat_count, local, 2 * qn, width), bf16),
            pltpu.VMEM((lat_count, local, 2 * qn, width), bf16),
            pltpu.VMEM((qn * bands, LANES), f32),
            pltpu.VMEM((kpt_count, groups, qn * bands, LANES), bf16),
            pltpu.VMEM((2, cells, bands * k_count), f32),
            pltpu.VMEM((2, bands, bands * k_count), f32),
            pltpu.VMEM((2 * blocks, 2 * cells * bands, lanes), bf16),
            pltpu.VMEM((k_count // span, tall, q_count * 2 * LANES), bf16),
            pltpu.VMEM((lanes // LANES, q_count * 2 * LANES, octets * LANES), bf16),
            dma((lat_count,)),
            dma((lat_count,)),
            dma((chips,)),
            dma((chips,)),
            dma((chips,)),
            dma((chips,)),
        ],
        compiler_params=pltpu.CompilerParams(collective_id=0, has_side_effects=True),
    )(
        rp_vectors,
        rp_weights,
        q_points,
        coarse,
        modes_rot,
        jnp.transpose(re_vectors),
        re_weights.reshape(1, cells),
        jnp.transpose(k_points),
        uk,
        ukq,
        keep_k,
        keep_kq,
    )


def solution(mesh):
    placed = (
        P(None, "lat", "kpt", None),
        P("lat", None),
        P("lat"),
        P(),
        P(),
        P(),
        P("kpt", None),
        P(),
        P(None, "kpt", None, None),
        P(None, None, "kpt", None, None),
        P("kpt", None),
        P(None, "kpt", None),
    )
    return jax.shard_map(
        functools.partial(per_device, mesh.shape["lat"], mesh.shape["kpt"]),
        mesh=mesh,
        in_specs=placed,
        out_specs=P(None, "kpt", None, "lat"),
        check_vma=False,
    )
```

```python
import functools

import jax
import jax.numpy as jnp
from jax import lax
from jax.experimental import pallas as pl
from jax.experimental.pallas import tpu as pltpu
from jax.sharding import PartitionSpec as P

two_pi = 6.283185307179586
f32 = jnp.float32
bf16 = jnp.bfloat16
i32 = jnp.int32
MESH = pl.DeviceIdType.MESH
LANES = 128


def up(value, step):
    return -(-value // step) * step


def iota(shape, axis):
    return lax.broadcasted_iota(i32, shape, axis)


def dot(a, b):
    return jnp.dot(a, b, preferred_element_type=f32)


def exchange(tiles, unit, axis=1):
    span = len(tiles)
    shape = next(t for t in tiles if t is not None).shape
    place = iota(shape, axis)
    bit = 1
    while bit < span:
        shift = unit * bit
        odd = (place & shift) != 0
        turned = list(tiles)
        for i in range(span):
            if i & bit:
                continue
            a, b = tiles[i], tiles[i | bit]
            if a is None:
                continue
            ahead = pltpu.roll(a, shape[axis] - shift, axis)
            if b is None:
                turned[i], turned[i | bit] = a, ahead
            else:
                turned[i] = jnp.where(odd, pltpu.roll(b, shift, axis), a)
                turned[i | bit] = jnp.where(odd, b, ahead)
        tiles = turned
        bit *= 2
    return tiles


def gather_kernel(
    lat_count,
    kpt_count,
    modes,
    qp_hbm,
    rpv_hbm,
    rpw_hbm,
    x_hbm,
    rot_hbm,
    rv_hbm,
    rw_hbm,
    kp_hbm,
    u_hbm,
    v_hbm,
    mk_hbm,
    mkq_hbm,
    acc,
    vb,
    qp,
    rpv,
    rpw,
    x_ref,
    rot_ref,
    rv_ref,
    rw_ref,
    kp_ref,
    u_ref,
    v_ref,
    mk_ref,
    mkq_ref,
    xs,
    wre,
    wim,
    part,
    recv,
    turned,
    gath,
    p2,
    u2,
    gs,
    loads,
    lat_send,
    lat_recv,
    chip_send,
    chip_recv,
    pair_send,
    pair_recv,
):
    given = (qp_hbm, rpv_hbm, rpw_hbm, x_hbm, rot_hbm, rv_hbm, rw_hbm, kp_hbm, u_hbm, v_hbm, mk_hbm, mkq_hbm)
    held = (qp, rpv, rpw, x_ref, rot_ref, rv_ref, rw_ref, kp_ref, u_ref, v_ref, mk_ref, mkq_ref)
    load = []
    for i in range(len(given)):
        load.append(pltpu.make_async_copy(given[i], held[i], loads.at[i]))
        load[i].start()
    lat = lax.axis_index("lat")
    kpt = lax.axis_index("kpt")
    chips = kpt_count // 2
    chip = kpt // 2
    core = kpt - 2 * chip
    pair = 2 * chip + 1 - core

    def lat_peer(step):
        return lax.rem(lat + step, lat_count)

    def chip_peer(step):
        return lax.rem(chip + step, chips)

    barrier = pltpu.get_barrier_semaphore()
    for step in range(1, lat_count):
        pl.semaphore_signal(barrier, inc=1, device_id=(lat_peer(step), kpt), device_id_type=MESH)
    for step in range(1, chips):
        pl.semaphore_signal(barrier, inc=1, device_id=(lat, 2 * chip_peer(step) + core), device_id_type=MESH)
    pl.semaphore_signal(barrier, inc=1, device_id=(lat, pair), device_id_type=MESH)

    q_count = rot_ref.shape[1]
    mode_count = rot_ref.shape[2]
    local = x_ref.shape[2]
    bands = mk_ref.shape[0]
    k_count = mk_ref.shape[1]
    width = bands * bands
    halves = width // LANES
    cells = rv_ref.shape[1]
    qn = part.shape[2] // 2
    span = LANES // bands
    quad = 16 // (halves * q_count)

    for copy in load[:5]:
        copy.wait()
    if q_count * modes != qn:
        wre[...] = jnp.zeros_like(wre)
        wim[...] = jnp.zeros_like(wim)
    for q in range(q_count):
        term = qp[q : q + 1, :] * rpv[...].astype(f32)
        argument = two_pi * (term[:, 0:1] + term[:, 1:2] + term[:, 2:3])
        argument = jnp.broadcast_to(argument, (1, mode_count))
        inverse = 1.0 / jnp.broadcast_to(rpw[...].astype(f32), (1, mode_count))
        pr = (jnp.cos(argument) * inverse).astype(bf16).astype(f32)
        pi = (jnp.sin(argument) * inverse).astype(bf16).astype(f32)
        mr = rot_ref[0, q].astype(f32).T
        mi = rot_ref[1, q].astype(f32).T
        wr = pr * mr - pi * mi
        wi = pr * mi + pi * mr
        for d in range(lat_count):
            rows = slice(d * modes, (d + 1) * modes)
            at = d * 2 * qn + q * modes
            wre[at : at + modes, :] = wr[rows]
            wim[at : at + modes, :] = -wi[rows]
            wre[at + qn : at + qn + modes, :] = wi[rows]
            wim[at + qn : at + qn + modes, :] = wr[rows]

    for c in range(2):
        x = x_ref[c, 0].astype(f32)
        for m in range(mode_count):
            for h in range(halves):
                at = (h * mode_count + m) * 2 * local + c * local
                lane = m * width + h * LANES
                xs[at : at + local, :] = x[:, lane : lane + LANES]

    def rows_of(c, e):
        return jnp.concatenate(
            [
                xs[pl.ds(h * mode_count * 2 * local + c * local + e, mode_count, stride=2 * local), :]
                for h in range(halves)
            ],
            axis=1,
        ).astype(bf16)

    left, right = wre[...].astype(bf16), wim[...].astype(bf16)
    for e in range(local):
        piece = (dot(left, rows_of(0, e)) + dot(right, rows_of(1, e))).astype(bf16)
        for d in range(lat_count):
            part[d, e] = piece[d * 2 * qn : (d + 1) * 2 * qn]

    pl.semaphore_wait(barrier, lat_count + chips - 1)
    first = []
    for step in range(1, lat_count):
        copy = pltpu.make_async_remote_copy(
            src_ref=part.at[lat_peer(step)],
            dst_ref=recv.at[lat],
            send_sem=lat_send.at[step],
            recv_sem=lat_recv.at[step],
            device_id=(lat_peer(step), kpt),
            device_id_type=MESH,
        )
        copy.start()
        first.append(copy)

    for copy in load[5:]:
        copy.wait()
    size = bands * k_count
    spread = iota((k_count, size), 1) - bands * iota((k_count, size), 0)
    spread = ((spread >= 0) & (spread < bands)).astype(f32).astype(bf16)
    eye = iota((cells, cells), 0) == iota((cells, cells), 1)

    def column(row):
        return jnp.sum(jnp.where(eye, row, 0.0), axis=1, keepdims=True)

    column_of = [column(rv_ref[i : i + 1, :].astype(f32)) for i in range(3)]
    argument = two_pi * (
        kp_ref[0:1, :] * column_of[0] + kp_ref[1:2, :] * column_of[1] + kp_ref[2:3, :] * column_of[2]
    )
    inverse = 1.0 / column(rw_ref[...].astype(f32))
    p2[0] = dot((jnp.cos(argument) * inverse).astype(bf16), spread)
    p2[1] = dot((jnp.sin(argument) * inverse).astype(bf16), spread)

    row = iota((width, size), 0)
    lane = iota((width, size), 1) & (bands - 1)
    pick = iota((bands, width), 1)
    order = iota((bands, width), 0)
    minor = (row & (bands - 1)) == lane
    major = (row // bands) == lane
    take_major = ((pick // bands) == order).astype(f32).astype(bf16)
    take_minor = ((pick & (bands - 1)) == order).astype(f32).astype(bf16)
    keep = jnp.concatenate([mk_ref[...].astype(f32)] * bands, axis=0)
    for c in range(2):
        wide = dot((u_ref[c].astype(f32) * keep).astype(bf16), spread)
        u2[c] = dot(take_major, jnp.where(minor, wide, 0.0).astype(bf16))
    blocks = gs.shape[0] // 2
    lanes = gs.shape[2]

    def grow(e, carry):
        pr, pi = p2[0, pl.ds(e, 1), :], p2[1, pl.ds(e, 1), :]
        re = (pr * u2[0] - pi * u2[1]).astype(bf16)
        im = pr * u2[1] + pi * u2[0]
        minus = (-im).astype(bf16)
        im = im.astype(bf16)
        at = pl.ds(pl.multiple_of(e * 2 * bands, bands), bands)
        below = pl.ds(pl.multiple_of(e * 2 * bands + bands, bands), bands)
        for t in range(blocks):
            cut = slice(t * lanes, (t + 1) * lanes)
            gs[t, at, :] = re[:, cut]
            gs[blocks + t, at, :] = im[:, cut]
            gs[t, below, :] = minus[:, cut]
            gs[blocks + t, below, :] = re[:, cut]
        return carry

    lax.fori_loop(0, cells, grow, 0)

    turn = []
    for q in range(q_count):
        keep = jnp.concatenate([mkq_ref[q].astype(f32)] * bands, axis=0)
        for c in range(2):
            wide = dot((v_ref[c, q].astype(f32) * keep).astype(bf16), spread)
            turn.append(dot(take_minor, jnp.where(major, wide, 0.0).astype(bf16)))
    tall = 2 * bands * span * q_count
    height = span // quad * halves * q_count * quad
    row = iota((tall, LANES), 0)
    at_q = row & (q_count - 1)
    at_k = ((row // (quad * halves * q_count)) & (span // quad - 1)) * quad + (
        (row // (halves * q_count)) & (quad - 1)
    )
    same = [(at_k == iota((tall, LANES), 1) // bands) & (at_q == q) for q in range(q_count)]
    row = iota((tall, 2 * bands), 0)
    band = ((row // q_count) & (halves - 1)) * span + ((row // height) & (span - 1))
    band = band + row // (tall // 2) * bands
    repeat = (band == iota((tall, 2 * bands), 1)).astype(f32).astype(bf16)
    for o in range(k_count // span):
        cut = slice(o * LANES, (o + 1) * LANES)
        for q in range(q_count):
            re, im = turn[2 * q][:, cut], turn[2 * q + 1][:, cut]
            both = [jnp.concatenate([re, -im], axis=0), jnp.concatenate([im, re], axis=0)]
            for c in range(2):
                wide = jnp.where(same[q], dot(repeat, both[c].astype(bf16)), 0.0)
                at = (q * 2 + c) * LANES
                vb[o, :, at : at + LANES] = wide.astype(bf16)

    for copy in first:
        copy.wait_recv()
    cut = span // 2
    for g in range(local // cut):
        rows = []
        for e in range(g * cut, (g + 1) * cut):
            total = part[lat, e].astype(f32)
            for step in range(1, lat_count):
                total = total + recv[lat_peer(step), e].astype(f32)
            rows += [total[:qn], total[qn:]]
        for h in range(halves):
            tiles = exchange([r[:, h * LANES : (h + 1) * LANES] for r in rows], bands)
            for a in range(span):
                turned[pl.ds(h * span + a, qn, stride=bands), :] = tiles[a]
        gath[kpt, g] = turned[...].astype(bf16)

    def apart(step, ordered):
        found = 0
        for z in range(chips):
            others = sorted((o for o in range(chips) if o != z), key=lambda o: abs(o - z))
            found = found + jnp.where(chip == z, ordered(others)[step], 0)
        return found

    second = []
    for step in range(chips - 1):
        copy = pltpu.make_async_remote_copy(
            src_ref=gath.at[kpt],
            dst_ref=gath.at[kpt],
            send_sem=chip_send.at[step],
            recv_sem=chip_recv.at[chip],
            device_id=(lat, 2 * apart(step, lambda o: o[::-1]) + core),
            device_id_type=MESH,
        )
        copy.start()
        second.append(copy)

    def arrival(ref, source, sem):
        return pltpu.make_async_remote_copy(
            src_ref=ref.at[source],
            dst_ref=ref.at[source],
            send_sem=chip_send.at[0],
            recv_sem=sem,
            device_id=(lat, pair),
            device_id_type=MESH,
        )

    def pass_on(step, source):
        copy = pltpu.make_async_remote_copy(
            src_ref=gath.at[source],
            dst_ref=gath.at[source],
            send_sem=pair_send.at[step],
            recv_sem=pair_recv.at[step],
            device_id=(lat, pair),
            device_id_type=MESH,
        )
        copy.start()
        return copy

    groups = local // cut
    deep = 2 * groups * LANES

    def add(z, first_time):
        left = jnp.concatenate([gath[2 * z + c, g] for c in range(2) for g in range(groups)], axis=1)
        at = pl.ds(pl.multiple_of(z * deep, deep), deep)
        for t in range(2 * blocks):
            term = dot(left, gs[t, at, :])
            acc[t] = term if first_time else acc[t] + term

    nearest = [chip] + [apart(step, lambda o: o) for step in range(chips - 1)]
    third = [pass_on(0, kpt)]
    for step in range(chips):
        if step + 1 < chips:
            source = 2 * nearest[step + 1] + core
        third[step].wait_recv()
        add(nearest[step], step == 0)
        if step + 1 < chips:
            arrival(gath, source, chip_recv.at[nearest[step + 1]]).wait_recv()
            third.append(pass_on(step + 1, source))
    for copy in first + second + third:
        copy.wait_send()


def couple_kernel(modes, q_count, bands, acc, vb, out_ref, rt, scr, sems):
    blocks = acc.shape[0] // 2
    near = acc.shape[2] // LANES
    span = LANES // bands
    width = bands * bands
    halves = width // LANES
    octets = -(-modes // span)
    quad = 16 // (halves * q_count)
    many = span // quad
    k_count = near * blocks * span
    held = modes * halves * q_count

    def leave(t):
        copies = []
        for c in range(2):
            rows = pl.ds(c * k_count + t * near * span, near * span)
            copies.append(
                pltpu.make_async_copy(scr.at[rows, :held], out_ref.at[rows], sems.at[t, c])
            )
        return copies

    def finish(t, carry):
        for o in range(near):
            for q in range(q_count):
                for c in range(2):
                    for s in range(octets):
                        tiles = []
                        for i in range(span):
                            m = s * span + i
                            at = (q * modes + m) * bands
                            tiles.append(
                                acc[c * blocks + t, at : at + bands, o * LANES : (o + 1) * LANES].astype(bf16)
                                if m < modes
                                else None
                            )
                        tiles = exchange(tiles, bands)
                        for i in range(span):
                            at = ((q * 2 + c) * span + i) * bands
                            rt[o, at : at + bands, s * LANES : (s + 1) * LANES] = tiles[i]
            done = dot(vb[t * near + o], rt[o])
            for c in range(2):
                for g in range(many):
                    found = []
                    for s in range(octets):
                        tiles = []
                        for i in range(span):
                            at = ((c * span + i) * many + g) * 16
                            tiles.append(done[at : at + 16, s * LANES : (s + 1) * LANES].astype(bf16))
                        found += exchange(tiles, bands)
                    for m in range(0, modes, quad):
                        tiles = [found[i] if i < modes else None for i in range(m, m + quad)]
                        tiles = exchange(tiles, halves * q_count, 0)
                        tall = min(quad, modes - m) * halves * q_count
                        for i in range(quad):
                            k = (t * near + o) * span + g * quad + i
                            at = m * halves * q_count
                            scr[c * k_count + k, at : at + tall, :] = tiles[i][:tall]
        for copy in leave(t):
            copy.start()
        return carry

    lax.fori_loop(0, blocks, finish, 0)
    for t in range(blocks):
        for copy in leave(t):
            copy.wait()


def per_device(
    lat_count,
    kpt_count,
    coarse,
    rp_vectors,
    rp_weights,
    re_vectors,
    re_weights,
    q_points,
    k_points,
    modes_rot,
    u_k,
    u_kq,
    mask_k,
    mask_kq,
):
    q_count = q_points.shape[0]
    k_count = k_points.shape[0]
    bands = u_k.shape[2]
    width = bands * bands
    local = coarse.shape[2]
    mode_count = coarse.shape[3] // width
    modes = mode_count // lat_count
    cells = re_vectors.shape[0]
    span = LANES // bands
    qn = up(q_count * modes, 8)
    groups = local // (span // 2)
    octets = -(-modes // span)
    chips = kpt_count // 2
    lanes = 2 * LANES
    blocks = bands * k_count // lanes
    assert coarse.shape[1] == 1 and local % (span // 2) == 0 and bands & (bands - 1) == 0

    uk = jnp.transpose(u_k, (0, 2, 3, 1)).reshape(2, width, k_count)
    ukq = jnp.transpose(u_kq, (0, 1, 3, 4, 2)).reshape(2, q_count, width, k_count)
    keep_k = jnp.transpose(mask_k)
    keep_kq = jnp.transpose(mask_kq, (0, 2, 1))

    anywhere = pl.BlockSpec(memory_space=pl.ANY)
    vmem = pl.BlockSpec(memory_space=pltpu.VMEM)
    dma = pltpu.SemaphoreType.DMA
    tall = span * q_count * 2 * bands
    rows = qn * bands
    inputs = (
        q_points,
        rp_vectors,
        rp_weights.reshape(1, 1),
        coarse,
        modes_rot,
        jnp.transpose(re_vectors),
        re_weights.reshape(1, cells),
        jnp.transpose(k_points),
        uk,
        ukq,
        keep_k,
        keep_kq,
    )
    acc, vb = pl.pallas_call(
        functools.partial(gather_kernel, lat_count, kpt_count, modes),
        in_specs=[anywhere] * len(inputs),
        out_specs=[vmem] * 2,
        out_shape=[
            pltpu.VMEM((2 * blocks, rows, lanes), f32),
            pltpu.VMEM((k_count // span, tall, q_count * 2 * LANES), bf16),
        ],
        scratch_shapes=[pltpu.VMEM(x.shape, x.dtype) for x in inputs]
        + [
            pltpu.VMEM((2 * local * mode_count * (width // LANES), LANES), f32),
            pltpu.VMEM((lat_count * 2 * qn, mode_count), f32),
            pltpu.VMEM((lat_count * 2 * qn, mode_count), f32),
            pltpu.VMEM((lat_count, local, 2 * qn, width), bf16),
            pltpu.VMEM((lat_count, local, 2 * qn, width), bf16),
            pltpu.VMEM((rows, LANES), f32),
            pltpu.VMEM((kpt_count, groups, rows, LANES), bf16),
            pltpu.VMEM((2, cells, bands * k_count), f32),
            pltpu.VMEM((2, bands, bands * k_count), f32),
            pltpu.VMEM((2 * blocks, 2 * cells * bands, lanes), bf16),
            dma((len(inputs),)),
            dma((lat_count,)),
            dma((lat_count,)),
            dma((chips,)),
            dma((chips,)),
            dma((chips,)),
            dma((chips,)),
        ],
        compiler_params=pltpu.CompilerParams(
            collective_id=0, has_side_effects=True, vmem_limit_bytes=48 * 1024 * 1024
        ),
    )(*inputs)
    count = modes * (width // LANES)
    held = count * q_count
    result = jax.ShapeDtypeStruct((2 * k_count, held, LANES), bf16)
    out = pl.pallas_call(
        functools.partial(couple_kernel, modes, q_count, bands),
        in_specs=[vmem] * 2,
        out_specs=anywhere,
        out_shape=result,
        scratch_shapes=[
            pltpu.VMEM((lanes // LANES, q_count * 2 * LANES, octets * LANES), bf16),
            pltpu.VMEM((2 * k_count, up(held, 16), LANES), bf16),
            dma((blocks, 2)),
        ],
        compiler_params=pltpu.CompilerParams(vmem_limit_bytes=16 * 1024 * 1024),
    )(acc, vb)
    out = out.reshape(2, k_count, count, q_count, LANES)
    return jnp.transpose(out, (0, 1, 3, 2, 4)).reshape(2, k_count, q_count, modes * width)


def solution(mesh):
    placed = (
        P(None, "lat", "kpt", None),
        P("lat", None),
        P("lat"),
        P(),
        P(),
        P(),
        P("kpt", None),
        P(),
        P(None, "kpt", None, None),
        P(None, None, "kpt", None, None),
        P("kpt", None),
        P(None, "kpt", None),
    )
    return jax.shard_map(
        functools.partial(per_device, mesh.shape["lat"], mesh.shape["kpt"]),
        mesh=mesh,
        in_specs=placed,
        out_specs=P(None, "kpt", None, "lat"),
        check_vma=False,
    )
```

```python
import functools

import jax
import jax.numpy as jnp
from jax import lax
from jax.experimental import pallas as pl
from jax.experimental.pallas import tpu as pltpu
from jax.sharding import PartitionSpec as P

two_pi = 6.283185307179586
f32 = jnp.float32
bf16 = jnp.bfloat16
i32 = jnp.int32
MESH = pl.DeviceIdType.MESH
LANES = 128


def up(value, step):
    return -(-value // step) * step


def iota(shape, axis):
    return lax.broadcasted_iota(i32, shape, axis)


def dot(a, b):
    return jnp.dot(a, b, preferred_element_type=f32)


def exchange(tiles, unit, axis=1):
    span = len(tiles)
    shape = next(t for t in tiles if t is not None).shape
    place = iota(shape, axis)
    skew = [t if i == 0 or t is None else pltpu.roll(t, i * unit, axis) for i, t in enumerate(tiles)]
    tiles = [skew[-i % span] for i in range(span)]
    bit = 1
    while bit < span:
        odd = (place & (unit * bit)) != 0
        turned = []
        for i in range(span):
            a, b = tiles[i], tiles[(i - bit) % span]
            turned.append(b if a is None else a if b is None else jnp.where(odd, b, a))
        tiles = turned
        bit *= 2
    return [t if i == 0 else pltpu.roll(t, shape[axis] - i * unit, axis) for i, t in enumerate(tiles)]


def gather_kernel(
    lat_count,
    kpt_count,
    modes,
    qp_hbm,
    rpv_hbm,
    rpw_hbm,
    x_hbm,
    rot_hbm,
    rv_hbm,
    rw_hbm,
    kp_hbm,
    u_hbm,
    v_hbm,
    mk_hbm,
    mkq_hbm,
    gath,
    gs,
    vb,
    qp,
    rpv,
    rpw,
    x_ref,
    rot_ref,
    rv_ref,
    rw_ref,
    kp_ref,
    u_ref,
    v_ref,
    mk_ref,
    mkq_ref,
    xs,
    wre,
    wim,
    part,
    recv,
    turned,
    p2,
    u2,
    loads,
    lat_send,
    lat_recv,
    chip_send,
    chip_recv,
    relay_send,
    pair_send,
    pair_recv,
):
    given = (qp_hbm, rpv_hbm, rpw_hbm, x_hbm, rot_hbm, rv_hbm, rw_hbm, kp_hbm, u_hbm, v_hbm, mk_hbm, mkq_hbm)
    held = (qp, rpv, rpw, x_ref, rot_ref, rv_ref, rw_ref, kp_ref, u_ref, v_ref, mk_ref, mkq_ref)
    load = []
    for i in range(len(given)):
        load.append(pltpu.make_async_copy(given[i], held[i], loads.at[i]))
        load[i].start()
    lat = lax.axis_index("lat")
    kpt = lax.axis_index("kpt")
    chips = kpt_count // 2
    chip = kpt // 2
    core = kpt - 2 * chip
    pair = 2 * chip + 1 - core

    def lat_peer(step):
        return lax.rem(lat + step, lat_count)

    def chip_peer(step):
        return lax.rem(chip + step, chips)

    barrier = pltpu.get_barrier_semaphore()
    for step in range(1, lat_count):
        pl.semaphore_signal(barrier, inc=1, device_id=(lat_peer(step), kpt), device_id_type=MESH)
    for step in range(1, chips):
        pl.semaphore_signal(barrier, inc=1, device_id=(lat, 2 * chip_peer(step) + core), device_id_type=MESH)
    pl.semaphore_signal(barrier, inc=1, device_id=(lat, pair), device_id_type=MESH)

    q_count = rot_ref.shape[1]
    mode_count = rot_ref.shape[2]
    local = x_ref.shape[2]
    bands = mk_ref.shape[0]
    k_count = mk_ref.shape[1]
    width = bands * bands
    halves = width // LANES
    cells = rv_ref.shape[1]
    sets = part.shape[0]
    qn = sets * 8
    span = LANES // bands
    quad = 16 // (halves * q_count)

    for copy in load[:5]:
        copy.wait()
    if q_count * modes != qn:
        wre[...] = jnp.zeros_like(wre)
        wim[...] = jnp.zeros_like(wim)
    for q in range(q_count):
        term = qp[q : q + 1, :] * rpv[...].astype(f32)
        argument = two_pi * (term[:, 0:1] + term[:, 1:2] + term[:, 2:3])
        argument = jnp.broadcast_to(argument, (1, mode_count))
        inverse = 1.0 / jnp.broadcast_to(rpw[...].astype(f32), (1, mode_count))
        pr = (jnp.cos(argument) * inverse).astype(bf16).astype(f32)
        pi = (jnp.sin(argument) * inverse).astype(bf16).astype(f32)
        mr = rot_ref[0, q].astype(f32).T
        mi = rot_ref[1, q].astype(f32).T
        wr = pr * mr - pi * mi
        wi = pr * mi + pi * mr
        for d in range(lat_count):
            done = 0
            while done < modes:
                first_row = q * modes + done
                take = min(8 - first_row % 8, modes - done)
                rows = slice(d * modes + done, d * modes + done + take)
                at = d * 2 * qn + first_row // 8 * 16 + first_row % 8
                wre[at : at + take, :] = wr[rows]
                wim[at : at + take, :] = -wi[rows]
                wre[at + 8 : at + 8 + take, :] = wi[rows]
                wim[at + 8 : at + 8 + take, :] = wr[rows]
                done += take

    for c in range(2):
        x = x_ref[c, 0].astype(f32)
        for m in range(mode_count):
            for h in range(halves):
                at = (h * mode_count + m) * 2 * local + c * local
                lane = m * width + h * LANES
                xs[at : at + local, :] = x[:, lane : lane + LANES]

    def rows_of(c, e):
        return jnp.concatenate(
            [
                xs[pl.ds(h * mode_count * 2 * local + c * local + e, mode_count, stride=2 * local), :]
                for h in range(halves)
            ],
            axis=1,
        ).astype(bf16)

    left, right = wre[...].astype(bf16), wim[...].astype(bf16)
    for e in range(local):
        piece = (dot(left, rows_of(0, e)) + dot(right, rows_of(1, e))).astype(bf16)
        for d in range(lat_count):
            for i in range(sets):
                at = d * 2 * qn + i * 16
                part[i, d, e] = piece[at : at + 16]

    pl.semaphore_wait(barrier, lat_count + chips - 1)
    first = [
        [
            pltpu.make_async_remote_copy(
                src_ref=part.at[i, lat_peer(step)],
                dst_ref=recv.at[i, lat],
                send_sem=lat_send.at[i, step],
                recv_sem=lat_recv.at[i, step],
                device_id=(lat_peer(step), kpt),
                device_id_type=MESH,
            )
            for step in range(1, lat_count)
        ]
        for i in range(sets)
    ]
    for copies in first:
        for copy in copies:
            copy.start()

    for copy in load[5:]:
        copy.wait()
    size = bands * k_count
    spread = iota((k_count, size), 1) - bands * iota((k_count, size), 0)
    spread = ((spread >= 0) & (spread < bands)).astype(f32).astype(bf16)
    eye = iota((cells, cells), 0) == iota((cells, cells), 1)

    def column(row):
        return jnp.sum(jnp.where(eye, row, 0.0), axis=1, keepdims=True)

    column_of = [column(rv_ref[i : i + 1, :].astype(f32)) for i in range(3)]
    argument = two_pi * (
        kp_ref[0:1, :] * column_of[0] + kp_ref[1:2, :] * column_of[1] + kp_ref[2:3, :] * column_of[2]
    )
    inverse = 1.0 / column(rw_ref[...].astype(f32))
    p2[0] = dot((jnp.cos(argument) * inverse).astype(bf16), spread)
    p2[1] = dot((jnp.sin(argument) * inverse).astype(bf16), spread)

    row = iota((width, size), 0)
    lane = iota((width, size), 1) & (bands - 1)
    pick = iota((bands, width), 1)
    order = iota((bands, width), 0)
    minor = (row & (bands - 1)) == lane
    major = (row // bands) == lane
    take_major = ((pick // bands) == order).astype(f32).astype(bf16)
    take_minor = ((pick & (bands - 1)) == order).astype(f32).astype(bf16)
    keep = jnp.concatenate([mk_ref[...].astype(f32)] * bands, axis=0)
    for c in range(2):
        wide = dot((u_ref[c].astype(f32) * keep).astype(bf16), spread)
        u2[c] = dot(take_major, jnp.where(minor, wide, 0.0).astype(bf16))
    blocks = gs.shape[0] // 2
    lanes = gs.shape[2]

    def grow(e, carry):
        pr, pi = p2[0, pl.ds(e, 1), :], p2[1, pl.ds(e, 1), :]
        re = (pr * u2[0] - pi * u2[1]).astype(bf16)
        im = pr * u2[1] + pi * u2[0]
        minus = (-im).astype(bf16)
        im = im.astype(bf16)
        at = pl.ds(pl.multiple_of(e * 2 * bands, bands), bands)
        below = pl.ds(pl.multiple_of(e * 2 * bands + bands, bands), bands)
        for t in range(blocks):
            cut = slice(t * lanes, (t + 1) * lanes)
            gs[t, at, :] = re[:, cut]
            gs[blocks + t, at, :] = im[:, cut]
            gs[t, below, :] = minus[:, cut]
            gs[blocks + t, below, :] = re[:, cut]
        return carry

    lax.fori_loop(0, cells, grow, 0)

    tall = 2 * bands * span * q_count
    height = span // quad * halves * q_count * quad
    row = iota((tall, LANES), 0)
    at_q = row & (q_count - 1)
    at_k = ((row // (quad * halves * q_count)) & (span // quad - 1)) * quad + (
        (row // (halves * q_count)) & (quad - 1)
    )
    same = [(at_k == iota((tall, LANES), 1) // bands) & (at_q == q) for q in range(q_count)]
    row = iota((tall, 2 * bands), 0)
    band = ((row // q_count) & (halves - 1)) * span + ((row // height) & (span - 1))
    band = band + row // (tall // 2) * bands
    repeat = (band == iota((tall, 2 * bands), 1)).astype(f32).astype(bf16)

    def lay(q):
        keep = jnp.concatenate([mkq_ref[q].astype(f32)] * bands, axis=0)
        turn = []
        for c in range(2):
            wide = dot((v_ref[c, q].astype(f32) * keep).astype(bf16), spread)
            turn.append(dot(take_minor, jnp.where(major, wide, 0.0).astype(bf16)))
        for o in range(k_count // span):
            re, im = (x[:, o * LANES : (o + 1) * LANES] for x in turn)
            both = [jnp.concatenate([re, -im], axis=0), jnp.concatenate([im, re], axis=0)]
            for c in range(2):
                wide = jnp.where(same[q], dot(repeat, both[c].astype(bf16)), 0.0)
                at = (q * 2 + c) * LANES
                vb[o, :, at : at + LANES] = wide.astype(bf16)

    def relayed(source, target):
        if chips < 3:
            return False
        return ((target == chips - 1) & (source == chips - 3)) | ((target == 0) & (source == 2))

    def apart(step):
        found = 0
        for z in range(chips):
            others = [o for o in range(chips) if o != z]
            between = {1: 2, chips - 2: chips - 3}.get(z) if chips > 2 else None
            others = sorted(others, key=lambda o: (abs(o - z), o != between))
            found = found + jnp.where(chip == z, others[step], 0)
        return found

    def over(source, i, target, send_sem, recv_sem):
        return pltpu.make_async_remote_copy(
            src_ref=gath.at[source, i],
            dst_ref=gath.at[source, i],
            send_sem=send_sem,
            recv_sem=recv_sem,
            device_id=(lat, target),
            device_id_type=MESH,
        )

    def outward(i, act):
        for down in (True, False):
            for z in reversed(range(chips)) if down else range(chips):
                ahead = (chip < z) if down else (chip > z)

                @pl.when(ahead & jnp.logical_not(relayed(chip, z)))
                def _():
                    act(over(kpt, i, 2 * z + core, chip_send.at[i, z], chip_recv.at[i, chip]))

    def onward(i, source, act):
        for n, (at, end, origin) in enumerate(((chips - 2, chips - 1, chips - 3), (1, 0, 2))):
            if chips < 3:
                continue

            @pl.when((chip == at) & (source == origin))
            def _():
                act(over(2 * source + core, i, 2 * end + core, relay_send.at[i, n], chip_recv.at[i, source]))

    def start(copy):
        copy.start()

    def sent(copy):
        copy.wait_send()

    third = []

    def pass_on(source, i, step):
        copy = over(source, i, pair, pair_send.at[i, step], pair_recv.at[i, step])
        copy.start()
        third.append(copy)

    cut = span // 2
    for i in range(sets):
        for copy in first[i]:
            copy.wait_recv()
        for g in range(local // cut):
            rows = []
            for e in range(g * cut, (g + 1) * cut):
                total = part[i, lat, e].astype(f32)
                for step in range(1, lat_count):
                    total = total + recv[i, lat_peer(step), e].astype(f32)
                rows += [total[:8], total[8:]]
            for h in range(halves):
                tiles = exchange([r[:, h * LANES : (h + 1) * LANES] for r in rows], bands)
                for a in range(span):
                    turned[pl.ds(h * span + a, 8, stride=bands), :] = tiles[a]
            gath[kpt, i, g] = turned[...].astype(bf16)
        outward(i, start)
        pass_on(kpt, i, chips - 1)

    waits = sorted(
        ((i + min(step, 1) + 0.1 * step, step, i) for step in range(chips - 1) for i in range(sets))
    )
    laid = 0
    for _, step, i in waits:
        source = apart(step)
        over(2 * source + core, i, pair, chip_send.at[i, 0], chip_recv.at[i, source]).wait_recv()
        onward(i, source, start)
        pass_on(2 * source + core, i, step)
        if i == 0 and step != 1 and laid < q_count:
            lay(laid)
            laid += 1
    for q in range(laid, q_count):
        lay(q)
    for copy in third:
        copy.wait_recv()
    for copies in first:
        for copy in copies:
            copy.wait_send()
    for copy in third:
        copy.wait_send()
    for i in range(sets):
        outward(i, sent)
        for step in range(chips - 1):
            onward(i, apart(step), sent)


def couple_kernel(modes, q_count, bands, gath, gs, vb, out_ref, rt, scr, sems):
    blocks = gs.shape[0] // 2
    near = gs.shape[2] // LANES
    span = LANES // bands
    width = bands * bands
    halves = width // LANES
    octets = -(-modes // span)
    quad = 16 // (halves * q_count)
    many = span // quad
    k_count = near * blocks * span
    held = modes * halves * q_count

    def leave(t):
        copies = []
        for c in range(2):
            rows = pl.ds(c * k_count + t * near * span, near * span)
            copies.append(
                pltpu.make_async_copy(scr.at[rows, :held], out_ref.at[rows], sems.at[t, c])
            )
        return copies

    def finish(t, carry):
        chunks, sets, groups = gath.shape[:3]
        left = jnp.concatenate(
            [
                jnp.concatenate([gath[j, i, g] for j in range(chunks) for g in range(groups)], axis=1)
                for i in range(sets)
            ],
            axis=0,
        )
        field = [dot(left, gs[c * blocks + t]).astype(bf16) for c in range(2)]
        for o in range(near):
            for q in range(q_count):
                for c in range(2):
                    for s in range(octets):
                        tiles = []
                        for i in range(span):
                            m = s * span + i
                            at = (q * modes + m) * bands
                            tiles.append(
                                field[c][at : at + bands, o * LANES : (o + 1) * LANES] if m < modes else None
                            )
                        tiles = exchange(tiles, bands)
                        for i in range(span):
                            at = ((q * 2 + c) * span + i) * bands
                            rt[o, s, at : at + bands, :] = tiles[i]
            right = jnp.concatenate([rt[o, s] for s in range(octets)], axis=1)
            done = dot(vb[t * near + o], right)
            for c in range(2):
                for g in range(many):
                    found = []
                    for s in range(octets):
                        tiles = []
                        for i in range(span):
                            at = ((c * span + i) * many + g) * 16
                            tiles.append(done[at : at + 16, s * LANES : (s + 1) * LANES].astype(bf16))
                        found += exchange(tiles, bands)
                    for m in range(0, modes, quad):
                        tiles = [found[i] if i < modes else None for i in range(m, m + quad)]
                        tiles = exchange(tiles, halves * q_count, 0)
                        tall = min(quad, modes - m) * halves * q_count
                        for i in range(quad):
                            k = (t * near + o) * span + g * quad + i
                            at = m * halves * q_count
                            scr[c * k_count + k, at : at + tall, :] = tiles[i][:tall]
        for copy in leave(t):
            copy.start()
        return carry

    lax.fori_loop(0, blocks, finish, 0)
    for t in range(blocks):
        for copy in leave(t):
            copy.wait()


def per_device(
    lat_count,
    kpt_count,
    coarse,
    rp_vectors,
    rp_weights,
    re_vectors,
    re_weights,
    q_points,
    k_points,
    modes_rot,
    u_k,
    u_kq,
    mask_k,
    mask_kq,
):
    q_count = q_points.shape[0]
    k_count = k_points.shape[0]
    bands = u_k.shape[2]
    width = bands * bands
    local = coarse.shape[2]
    mode_count = coarse.shape[3] // width
    modes = mode_count // lat_count
    cells = re_vectors.shape[0]
    span = LANES // bands
    qn = up(q_count * modes, 8)
    sets = qn // 8
    groups = local // (span // 2)
    octets = -(-modes // span)
    chips = kpt_count // 2
    lanes = 2 * LANES
    blocks = bands * k_count // lanes
    assert coarse.shape[1] == 1 and local % (span // 2) == 0 and bands & (bands - 1) == 0

    uk = jnp.transpose(u_k, (0, 2, 3, 1)).reshape(2, width, k_count)
    ukq = jnp.transpose(u_kq, (0, 1, 3, 4, 2)).reshape(2, q_count, width, k_count)
    keep_k = jnp.transpose(mask_k)
    keep_kq = jnp.transpose(mask_kq, (0, 2, 1))

    anywhere = pl.BlockSpec(memory_space=pltpu.HBM)
    vmem = pl.BlockSpec(memory_space=pltpu.VMEM)
    dma = pltpu.SemaphoreType.DMA
    tall = span * q_count * 2 * bands
    inputs = (
        q_points,
        rp_vectors,
        rp_weights.reshape(1, 1),
        coarse,
        modes_rot,
        jnp.transpose(re_vectors),
        re_weights.reshape(1, cells),
        jnp.transpose(k_points),
        uk,
        ukq,
        keep_k,
        keep_kq,
    )
    kept = (
        2 * kpt_count * sets * groups * 8 * bands * LANES
        + 2 * 2 * blocks * 2 * cells * bands * lanes
        + 2 * (k_count // span) * tall * q_count * 2 * LANES
    )
    parts = pl.pallas_call(
        functools.partial(gather_kernel, lat_count, kpt_count, modes),
        in_specs=[anywhere] * len(inputs),
        out_specs=[vmem] * 3,
        out_shape=[
            pltpu.VMEM((kpt_count, sets, groups, 8 * bands, LANES), bf16),
            pltpu.VMEM((2 * blocks, 2 * cells * bands, lanes), bf16),
            pltpu.VMEM((k_count // span, tall, q_count * 2 * LANES), bf16),
        ],
        scratch_shapes=[pltpu.VMEM(x.shape, x.dtype) for x in inputs]
        + [
            pltpu.VMEM((2 * local * mode_count * (width // LANES), LANES), f32),
            pltpu.VMEM((lat_count * 2 * qn, mode_count), f32),
            pltpu.VMEM((lat_count * 2 * qn, mode_count), f32),
            pltpu.VMEM((sets, lat_count, local, 16, width), bf16),
            pltpu.VMEM((sets, lat_count, local, 16, width), bf16),
            pltpu.VMEM((8 * bands, LANES), f32),
            pltpu.VMEM((2, cells, bands * k_count), f32),
            pltpu.VMEM((2, bands, bands * k_count), f32),
            dma((len(inputs),)),
            dma((sets, lat_count)),
            dma((sets, lat_count)),
            dma((sets, chips)),
            dma((sets, chips)),
            dma((sets, 2)),
            dma((sets, chips)),
            dma((sets, chips)),
        ],
        compiler_params=pltpu.CompilerParams(
            collective_id=0, has_side_effects=True, vmem_limit_bytes=63 * 1024 * 1024 - kept
        ),
    )(*inputs)
    count = modes * (width // LANES)
    held = count * q_count
    result = jax.ShapeDtypeStruct((2 * k_count, held, LANES), bf16)
    out = pl.pallas_call(
        functools.partial(couple_kernel, modes, q_count, bands),
        in_specs=[vmem] * 3,
        out_specs=anywhere,
        out_shape=result,
        scratch_shapes=[
            pltpu.VMEM((lanes // LANES, octets, q_count * 2 * LANES, LANES), bf16),
            pltpu.VMEM((2 * k_count, up(held, 16), LANES), bf16),
            dma((blocks, 2)),
        ],
        compiler_params=pltpu.CompilerParams(vmem_limit_bytes=40 * 1024 * 1024),
    )(*parts)
    out = out.reshape(2, k_count, count, q_count, LANES)
    return jnp.transpose(out, (0, 1, 3, 2, 4)).reshape(2, k_count, q_count, modes * width)


def solution(mesh):
    placed = (
        P(None, "lat", "kpt", None),
        P("lat", None),
        P("lat"),
        P(),
        P(),
        P(),
        P("kpt", None),
        P(),
        P(None, "kpt", None, None),
        P(None, None, "kpt", None, None),
        P("kpt", None),
        P(None, "kpt", None),
    )
    return jax.shard_map(
        functools.partial(per_device, mesh.shape["lat"], mesh.shape["kpt"]),
        mesh=mesh,
        in_specs=placed,
        out_specs=P(None, "kpt", None, "lat"),
        check_vma=False,
    )
```

```python
import functools
import math

import jax
import jax.numpy as jnp
from jax import lax
from jax.experimental import pallas as pl
from jax.experimental.pallas import tpu as pltpu
from jax.sharding import PartitionSpec as P

two_pi = 6.283185307179586
f32 = jnp.float32
bf16 = jnp.bfloat16
i32 = jnp.int32
MESH = pl.DeviceIdType.MESH
LANES = 128


def up(value, step):
    return -(-value // step) * step


def iota(shape, axis):
    return lax.broadcasted_iota(i32, shape, axis)


def dot(a, b):
    return jnp.dot(a, b, preferred_element_type=f32)


def exchange(tiles, unit, axis=1):
    span = len(tiles)
    shape = next(t for t in tiles if t is not None).shape
    place = iota(shape, axis)
    skew = [t if i == 0 or t is None else pltpu.roll(t, i * unit, axis) for i, t in enumerate(tiles)]
    tiles = [skew[-i % span] for i in range(span)]
    bit = 1
    while bit < span:
        odd = (place & (unit * bit)) != 0
        turned = []
        for i in range(span):
            a, b = tiles[i], tiles[(i - bit) % span]
            turned.append(b if a is None else a if b is None else jnp.where(odd, b, a))
        tiles = turned
        bit *= 2
    return [t if i == 0 else pltpu.roll(t, shape[axis] - i * unit, axis) for i, t in enumerate(tiles)]


def cell_sum(t, sets, gath, gs):
    chunks, _, groups = gath.shape[:3]
    left = jnp.concatenate(
        [jnp.concatenate([gath[j, i, g] for j in range(chunks) for g in range(groups)], axis=1) for i in sets],
        axis=0,
    )
    blocks = gs.shape[0] // 2
    return tuple(dot(left, gs[c * blocks + t]).astype(bf16) for c in range(2))


def finish(t, field, modes, q_count, bands, octets, rest, gs, vb, rt, scr):
    blocks = gs.shape[0] // 2
    near = gs.shape[2] // LANES
    span = LANES // bands
    halves = bands * bands // LANES
    quad = 16 // (halves * q_count)
    many = span // quad
    k_count = near * blocks * span
    last = modes // 8 * q_count
    sets = [j * q_count + q for j in octets for q in range(q_count)] + ([last] if rest else [])
    for c in range(2):
        for o in range(near):
            for n in range(len(sets)):
                tiles = []
                for i in range(8):
                    at = (n * 8 + i) * bands
                    tiles.append(field[c][at : at + bands, o * LANES : (o + 1) * LANES])
                for i, tile in enumerate(exchange(tiles, bands)):
                    at = (c * span + i) * bands
                    rt[o, n, at : at + bands, :] = tile
    turn = iota((16, LANES), 0) & (q_count - 1)

    def choose(tiles):
        tile = tiles[0]
        for q in range(1, q_count):
            tile = jnp.where(turn == q, tiles[q], tile)
        return tile

    for o in range(near):
        right = jnp.concatenate([rt[o, n] for n in range(len(sets))], axis=1)
        done = dot(vb[t * near + o], right)
        for c in range(2):
            for g in range(many):
                base = (c * many + g) * span * 16

                def tile(n, i):
                    at = base + i * 16
                    return done[at : at + 16, n * LANES : (n + 1) * LANES].astype(bf16)

                found = []
                for j in range(len(octets)):
                    found += exchange(
                        [choose([tile(j * q_count + q, i) for q in range(q_count)]) for i in range(span)], bands
                    )
                if rest:
                    tiles = exchange([tile(len(sets) - 1, i) for i in range(span)], bands)
                    found += [choose([tiles[q * rest + i] for q in range(q_count)]) for i in range(rest)]
                for m in range(0, len(found), quad):
                    tiles = (found[m : m + quad] + [None] * quad)[:quad]
                    tiles = exchange(tiles, halves * q_count, 0)
                    at = m * halves * q_count
                    tall = min(quad, len(found) - m) * halves * q_count
                    for i in range(quad):
                        k = (t * near + o) * span + g * quad + i
                        scr[c * k_count + k, at : at + tall, :] = tiles[i][:tall]


def gather_kernel(
    lat_count,
    kpt_count,
    modes,
    qp_hbm,
    rpv_hbm,
    rpw_hbm,
    x_hbm,
    rot_hbm,
    rv_hbm,
    rw_hbm,
    kp_hbm,
    u_hbm,
    v_hbm,
    mk_hbm,
    mkq_hbm,
    gath,
    gs,
    vb,
    qp,
    rpv,
    rpw,
    x_ref,
    rot_ref,
    rv_ref,
    rw_ref,
    kp_ref,
    u_ref,
    v_ref,
    mk_ref,
    mkq_ref,
    xs,
    wre,
    wim,
    part,
    recv,
    turned,
    p2,
    u2,
    v2,
    loads,
    lat_send,
    lat_recv,
    chip_send,
    chip_recv,
    relay_send,
    pair_send,
    pair_recv,
):
    given = (qp_hbm, rpv_hbm, rpw_hbm, x_hbm, rot_hbm, rv_hbm, rw_hbm, kp_hbm, u_hbm, v_hbm, mk_hbm, mkq_hbm)
    held = (qp, rpv, rpw, x_ref, rot_ref, rv_ref, rw_ref, kp_ref, u_ref, v_ref, mk_ref, mkq_ref)
    load = []
    for i in range(len(given)):
        load.append(pltpu.make_async_copy(given[i], held[i], loads.at[i]))
        load[i].start()
    lat = lax.axis_index("lat")
    kpt = lax.axis_index("kpt")
    chips = kpt_count // 2
    chip = kpt // 2
    core = kpt - 2 * chip
    pair = 2 * chip + 1 - core

    def lat_peer(step):
        return lax.rem(lat + step, lat_count)

    def chip_peer(step):
        return lax.rem(chip + step, chips)

    barrier = pltpu.get_barrier_semaphore()
    for step in range(1, lat_count):
        pl.semaphore_signal(barrier, inc=1, device_id=(lat_peer(step), kpt), device_id_type=MESH)
    for step in range(1, chips):
        pl.semaphore_signal(barrier, inc=1, device_id=(lat, 2 * chip_peer(step) + core), device_id_type=MESH)
    pl.semaphore_signal(barrier, inc=1, device_id=(lat, pair), device_id_type=MESH)

    q_count = rot_ref.shape[1]
    mode_count = rot_ref.shape[2]
    local = x_ref.shape[2]
    bands = mk_ref.shape[0]
    k_count = mk_ref.shape[1]
    width = bands * bands
    halves = width // LANES
    cells = rv_ref.shape[1]
    sets = part.shape[0]
    qn = sets * 8
    span = LANES // bands
    quad = 16 // (halves * q_count)

    for copy in load[:5]:
        copy.wait()
    if q_count * modes != qn:
        wre[...] = jnp.zeros_like(wre)
        wim[...] = jnp.zeros_like(wim)
    for q in range(q_count):
        term = qp[q : q + 1, :] * rpv[...].astype(f32)
        argument = two_pi * (term[:, 0:1] + term[:, 1:2] + term[:, 2:3])
        argument = jnp.broadcast_to(argument, (1, mode_count))
        inverse = 1.0 / jnp.broadcast_to(rpw[...].astype(f32), (1, mode_count))
        pr = (jnp.cos(argument) * inverse).astype(bf16).astype(f32)
        pi = (jnp.sin(argument) * inverse).astype(bf16).astype(f32)
        mr = rot_ref[0, q].astype(f32).T
        mi = rot_ref[1, q].astype(f32).T
        wr = pr * mr - pi * mi
        wi = pr * mi + pi * mr
        for d in range(lat_count):
            rest = modes % 8
            for n in range(0, modes, 8):
                take = min(8, modes - n)
                rows = slice(d * modes + n, d * modes + n + take)
                at = d * 2 * qn + (n // 8 * q_count + q) * 16
                if take == rest:
                    at = d * 2 * qn + n // 8 * q_count * 16 + q * rest
                wre[at : at + take, :] = wr[rows]
                wim[at : at + take, :] = -wi[rows]
                wre[at + 8 : at + 8 + take, :] = wi[rows]
                wim[at + 8 : at + 8 + take, :] = wr[rows]

    for c in range(2):
        x = x_ref[c, 0].astype(f32)
        for m in range(mode_count):
            for h in range(halves):
                at = (h * mode_count + m) * 2 * local + c * local
                lane = m * width + h * LANES
                xs[at : at + local, :] = x[:, lane : lane + LANES]

    def rows_of(c, e):
        return jnp.concatenate(
            [
                xs[pl.ds(h * mode_count * 2 * local + c * local + e, mode_count, stride=2 * local), :]
                for h in range(halves)
            ],
            axis=1,
        ).astype(bf16)

    left, right = wre[...].astype(bf16), wim[...].astype(bf16)
    for e in range(local):
        piece = (dot(left, rows_of(0, e)) + dot(right, rows_of(1, e))).astype(bf16)
        for d in range(lat_count):
            for i in range(sets):
                at = d * 2 * qn + i * 16
                part[i, d, e] = piece[at : at + 16]

    pl.semaphore_wait(barrier, lat_count + chips - 1)
    first = [
        [
            pltpu.make_async_remote_copy(
                src_ref=part.at[i, lat_peer(step)],
                dst_ref=recv.at[i, lat],
                send_sem=lat_send.at[i, step],
                recv_sem=lat_recv.at[i, step],
                device_id=(lat_peer(step), kpt),
                device_id_type=MESH,
            )
            for step in range(1, lat_count)
        ]
        for i in range(sets)
    ]
    for copies in first:
        for copy in copies:
            copy.start()

    for copy in load[5:]:
        copy.wait()
    size = bands * k_count
    spread = iota((k_count, size), 1) - bands * iota((k_count, size), 0)
    spread = ((spread >= 0) & (spread < bands)).astype(f32).astype(bf16)
    eye = iota((cells, cells), 0) == iota((cells, cells), 1)

    def column(row):
        return jnp.sum(jnp.where(eye, row, 0.0), axis=1, keepdims=True)

    column_of = [column(rv_ref[i : i + 1, :].astype(f32)) for i in range(3)]
    argument = two_pi * (
        kp_ref[0:1, :] * column_of[0] + kp_ref[1:2, :] * column_of[1] + kp_ref[2:3, :] * column_of[2]
    )
    inverse = 1.0 / column(rw_ref[...].astype(f32))
    p2[0] = dot((jnp.cos(argument) * inverse).astype(bf16), spread)
    p2[1] = dot((jnp.sin(argument) * inverse).astype(bf16), spread)

    row = iota((width, size), 0)
    lane = iota((width, size), 1) & (bands - 1)
    pick = iota((bands, width), 1)
    order = iota((bands, width), 0)
    minor = (row & (bands - 1)) == lane
    major = (row // bands) == lane
    take_major = ((pick // bands) == order).astype(f32).astype(bf16)
    take_minor = ((pick & (bands - 1)) == order).astype(f32).astype(bf16)
    keep = jnp.concatenate([mk_ref[...].astype(f32)] * bands, axis=0)
    for c in range(2):
        wide = dot((u_ref[c].astype(f32) * keep).astype(bf16), spread)
        u2[c] = dot(take_major, jnp.where(minor, wide, 0.0).astype(bf16))
    blocks = gs.shape[0] // 2
    lanes = gs.shape[2]

    def grow(e, carry):
        pr, pi = p2[0, pl.ds(e, 1), :], p2[1, pl.ds(e, 1), :]
        re = (pr * u2[0] - pi * u2[1]).astype(bf16)
        im = pr * u2[1] + pi * u2[0]
        minus = (-im).astype(bf16)
        im = im.astype(bf16)
        at = pl.ds(pl.multiple_of(e * 2 * bands, bands), bands)
        below = pl.ds(pl.multiple_of(e * 2 * bands + bands, bands), bands)
        for t in range(blocks):
            cut = slice(t * lanes, (t + 1) * lanes)
            gs[t, at, :] = re[:, cut]
            gs[blocks + t, at, :] = im[:, cut]
            gs[t, below, :] = minus[:, cut]
            gs[blocks + t, below, :] = re[:, cut]
        return carry

    lax.fori_loop(0, cells, grow, 0)

    tall = 2 * bands * span * q_count

    def lay(stage):
        if stage == 0:
            for q in range(q_count):
                keep = jnp.concatenate([mkq_ref[q].astype(f32)] * bands, axis=0)
                turn = []
                for c in range(2):
                    wide = dot((v_ref[c, q].astype(f32) * keep).astype(bf16), spread)
                    turn.append(dot(take_minor, jnp.where(major, wide, 0.0).astype(bf16)).astype(bf16))
                at = q * 2 * bands
                v2[0, at : at + bands, :], v2[0, at + bands : at + 2 * bands, :] = turn[0], -turn[1]
                v2[1, at : at + bands, :], v2[1, at + bands : at + 2 * bands, :] = turn[1], turn[0]
            return
        row = iota((tall, LANES), 0)
        at_k = ((row // (span * 16)) & (span // quad - 1)) * quad + ((row // (halves * q_count)) & (quad - 1))
        same = at_k == iota((tall, LANES), 1) // bands
        row = iota((tall, q_count * 2 * bands), 0)
        band = ((row // q_count) & (halves - 1)) * span + ((row // 16) & (span - 1))
        band = ((row & (q_count - 1)) * 2 + row // (tall // 2)) * bands + band
        repeat = (band == iota((tall, q_count * 2 * bands), 1)).astype(f32).astype(bf16)
        for o in range(k_count // span):
            for c in range(2):
                wide = dot(repeat, v2[c, :, o * LANES : (o + 1) * LANES])
                vb[o, :, c * LANES : (c + 1) * LANES] = jnp.where(same, wide, 0.0).astype(bf16)

    def relayed(source, target):
        if chips < 3:
            return False
        return ((target == chips - 1) & (source == chips - 3)) | ((target == 0) & (source == 2))

    def apart(step):
        found = 0
        for z in range(chips):
            others = [o for o in range(chips) if o != z]
            between = {1: 2, chips - 2: chips - 3}.get(z) if chips > 2 else None
            others = sorted(others, key=lambda o: (abs(o - z), o != between))
            found = found + jnp.where(chip == z, others[step], 0)
        return found

    def over(source, i, target, send_sem, recv_sem):
        return pltpu.make_async_remote_copy(
            src_ref=gath.at[source, i],
            dst_ref=gath.at[source, i],
            send_sem=send_sem,
            recv_sem=recv_sem,
            device_id=(lat, target),
            device_id_type=MESH,
        )

    def outward(i, act):
        for down in (True, False):
            for z in reversed(range(chips)) if down else range(chips):
                ahead = (chip < z) if down else (chip > z)

                @pl.when(ahead & jnp.logical_not(relayed(chip, z)))
                def _():
                    act(over(kpt, i, 2 * z + core, chip_send.at[i, z], chip_recv.at[i, chip]))

    def onward(i, source, act):
        for n, (at, end, origin) in enumerate(((chips - 2, chips - 1, chips - 3), (1, 0, 2))):
            if chips < 3:
                continue

            @pl.when((chip == at) & (source == origin))
            def _():
                act(over(2 * source + core, i, 2 * end + core, relay_send.at[i, n], chip_recv.at[i, source]))

    def start(copy):
        copy.start()

    def sent(copy):
        copy.wait_send()

    third = []

    def pass_on(source, i, step):
        copy = over(source, i, pair, pair_send.at[i, step], pair_recv.at[i, step])
        copy.start()
        third.append(copy)

    cut = span // 2
    for i in range(sets):
        for copy in first[i]:
            copy.wait_recv()
        for g in range(local // cut):
            rows = []
            for e in range(g * cut, (g + 1) * cut):
                total = part[i, lat, e].astype(f32)
                for step in range(1, lat_count):
                    total = total + recv[i, lat_peer(step), e].astype(f32)
                rows += [total[:8], total[8:]]
            for h in range(halves):
                tiles = exchange([r[:, h * LANES : (h + 1) * LANES] for r in rows], bands)
                for a in range(span):
                    turned[pl.ds(h * span + a, 8, stride=bands), :] = tiles[a]
            gath[kpt, i, g] = turned[...].astype(bf16)
        outward(i, start)
        pass_on(kpt, i, chips - 1)

    waits = sorted(
        ((i + min(step, 1) + 0.1 * step, step, i) for step in range(chips - 1) for i in range(sets))
    )
    stage = 0
    for _, step, i in waits:
        source = apart(step)
        over(2 * source + core, i, pair, chip_send.at[i, 0], chip_recv.at[i, source]).wait_recv()
        onward(i, source, start)
        pass_on(2 * source + core, i, step)
        if stage < 2 and i == 0 and step != 1:
            lay(stage)
            stage += 1
    while stage < 2:
        lay(stage)
        stage += 1
    for copy in third:
        copy.wait_recv()
    for copies in first:
        for copy in copies:
            copy.wait_send()
    for copy in third:
        copy.wait_send()
    for i in range(sets):
        outward(i, sent)
        for step in range(chips - 1):
            onward(i, apart(step), sent)


def couple_kernel(modes, q_count, bands, gath, gs, vb, out_ref, rt, scr, sems):
    blocks = gs.shape[0] // 2
    span = LANES // bands
    near = gs.shape[2] // LANES
    k_count = near * blocks * span
    held = out_ref.shape[1]
    sets = range(gath.shape[1])

    def leave(t):
        copies = []
        for c in range(2):
            rows = pl.ds(c * k_count + t * near * span, near * span)
            copies.append(pltpu.make_async_copy(scr.at[rows, :held], out_ref.at[rows], sems.at[t, c]))
        return copies

    def step(t, field):
        ahead = cell_sum(jnp.minimum(t + 1, blocks - 1), sets, gath, gs)
        finish(t, field, modes, q_count, bands, range(modes // 8), modes % 8, gs, vb, rt, scr)
        for copy in leave(t):
            copy.start()
        return ahead

    lax.fori_loop(0, blocks, step, cell_sum(0, sets, gath, gs))
    for t in range(blocks):
        for copy in leave(t):
            copy.wait()


def per_device(
    lat_count,
    kpt_count,
    coarse,
    rp_vectors,
    rp_weights,
    re_vectors,
    re_weights,
    q_points,
    k_points,
    modes_rot,
    u_k,
    u_kq,
    mask_k,
    mask_kq,
):
    q_count = q_points.shape[0]
    k_count = k_points.shape[0]
    bands = u_k.shape[2]
    width = bands * bands
    local = coarse.shape[2]
    mode_count = coarse.shape[3] // width
    modes = mode_count // lat_count
    cells = re_vectors.shape[0]
    span = LANES // bands
    qn = modes // 8 * 8 * q_count + up(modes % 8 * q_count, 8)
    sets = qn // 8
    groups = local // (span // 2)
    octets = -(-modes // span)
    chips = kpt_count // 2
    lanes = 2 * LANES
    blocks = bands * k_count // lanes
    assert coarse.shape[1] == 1 and local % (span // 2) == 0 and bands & (bands - 1) == 0

    uk = jnp.transpose(u_k, (0, 2, 3, 1)).reshape(2, width, k_count)
    ukq = jnp.transpose(u_kq, (0, 1, 3, 4, 2)).reshape(2, q_count, width, k_count)
    keep_k = jnp.transpose(mask_k)
    keep_kq = jnp.transpose(mask_kq, (0, 2, 1))

    anywhere = pl.BlockSpec(memory_space=pltpu.HBM)
    vmem = pl.BlockSpec(memory_space=pltpu.VMEM)
    dma = pltpu.SemaphoreType.DMA
    tall = span * q_count * 2 * bands
    inputs = (
        q_points,
        rp_vectors,
        rp_weights.reshape(1, 1),
        coarse,
        modes_rot,
        jnp.transpose(re_vectors),
        re_weights.reshape(1, cells),
        jnp.transpose(k_points),
        uk,
        ukq,
        keep_k,
        keep_kq,
    )
    count = modes * (width // LANES)
    held = count * q_count
    shapes = [
        ((kpt_count, sets, groups, 8 * bands, LANES), bf16),
        ((2 * blocks, 2 * cells * bands, lanes), bf16),
        ((k_count // span, tall, 2 * LANES), bf16),
    ]
    kept = sum(2 * math.prod(shape) for shape, _ in shapes)
    parts = pl.pallas_call(
        functools.partial(gather_kernel, lat_count, kpt_count, modes),
        in_specs=[anywhere] * len(inputs),
        out_specs=[vmem] * len(shapes),
        out_shape=[pltpu.VMEM(shape, dtype) for shape, dtype in shapes],
        scratch_shapes=[pltpu.VMEM(x.shape, x.dtype) for x in inputs]
        + [
            pltpu.VMEM((2 * local * mode_count * (width // LANES), LANES), f32),
            pltpu.VMEM((lat_count * 2 * qn, mode_count), f32),
            pltpu.VMEM((lat_count * 2 * qn, mode_count), f32),
            pltpu.VMEM((sets, lat_count, local, 16, width), bf16),
            pltpu.VMEM((sets, lat_count, local, 16, width), bf16),
            pltpu.VMEM((8 * bands, LANES), f32),
            pltpu.VMEM((2, cells, bands * k_count), f32),
            pltpu.VMEM((2, bands, bands * k_count), f32),
            pltpu.VMEM((2, q_count * 2 * bands, bands * k_count), bf16),
            dma((len(inputs),)),
            dma((sets, lat_count)),
            dma((sets, lat_count)),
            dma((sets, chips)),
            dma((sets, chips)),
            dma((sets, 2)),
            dma((sets, chips)),
            dma((sets, chips)),
        ],
        compiler_params=pltpu.CompilerParams(
            collective_id=0, has_side_effects=True, vmem_limit_bytes=63 * 1024 * 1024 - kept
        ),
    )(*inputs)
    result = jax.ShapeDtypeStruct((2 * k_count, held, LANES), bf16)
    out = pl.pallas_call(
        functools.partial(couple_kernel, modes, q_count, bands),
        in_specs=[vmem] * len(parts),
        out_specs=anywhere,
        out_shape=result,
        scratch_shapes=[
            pltpu.VMEM((lanes // LANES, sets, 2 * LANES, LANES), bf16),
            pltpu.VMEM((2 * k_count, up(held, 16), LANES), bf16),
            dma((blocks, 2)),
        ],
        compiler_params=pltpu.CompilerParams(vmem_limit_bytes=40 * 1024 * 1024),
    )(*parts)
    out = out.reshape(2, k_count, count, q_count, LANES)
    return jnp.transpose(out, (0, 1, 3, 2, 4)).reshape(2, k_count, q_count, modes * width)


def solution(mesh):
    placed = (
        P(None, "lat", "kpt", None),
        P("lat", None),
        P("lat"),
        P(),
        P(),
        P(),
        P("kpt", None),
        P(),
        P(None, "kpt", None, None),
        P(None, None, "kpt", None, None),
        P("kpt", None),
        P(None, "kpt", None),
    )
    return jax.shard_map(
        functools.partial(per_device, mesh.shape["lat"], mesh.shape["kpt"]),
        mesh=mesh,
        in_specs=placed,
        out_specs=P(None, "kpt", None, "lat"),
        check_vma=False,
    )
```

```python
import functools
import math

import jax
import jax.numpy as jnp
from jax import lax
from jax.experimental import pallas as pl
from jax.experimental.pallas import tpu as pltpu
from jax.sharding import PartitionSpec as P

two_pi = 6.283185307179586
f32 = jnp.float32
bf16 = jnp.bfloat16
i32 = jnp.int32
MESH = pl.DeviceIdType.MESH
LANES = 128


def up(value, step):
    return -(-value // step) * step


def iota(shape, axis):
    return lax.broadcasted_iota(i32, shape, axis)


def dot(a, b):
    return jnp.dot(a, b, preferred_element_type=f32)


def exchange(tiles, unit, axis=1):
    span = len(tiles)
    shape = next(t for t in tiles if t is not None).shape
    place = iota(shape, axis)
    skew = [t if i == 0 or t is None else pltpu.roll(t, i * unit, axis) for i, t in enumerate(tiles)]
    tiles = [skew[-i % span] for i in range(span)]
    bit = 1
    while bit < span:
        odd = (place & (unit * bit)) != 0
        turned = []
        for i in range(span):
            a, b = tiles[i], tiles[(i - bit) % span]
            turned.append(b if a is None else a if b is None else jnp.where(odd, b, a))
        tiles = turned
        bit *= 2
    return [t if i == 0 else pltpu.roll(t, shape[axis] - i * unit, axis) for i, t in enumerate(tiles)]


def apart(chip, chips, step):
    found = 0
    for z in range(chips):
        others = sorted((o for o in range(chips) if o != z), key=lambda o: abs(o - z))
        found = found + jnp.where(chip == z, others[step], 0)
    return found


def cell_sum(t, some, gath, gs):
    _, sets, groups = gath.shape[:3]
    deep = 2 * groups * LANES
    left = jnp.concatenate(
        [
            jnp.concatenate([gath[2 * z + c, i, g] for z in some for c in range(2) for g in range(groups)], axis=1)
            for i in range(sets)
        ],
        axis=0,
    )
    right = [gs[t, pl.ds(pl.multiple_of(z * deep, deep), deep), :] for z in some]
    return dot(left, jnp.concatenate(right, axis=0))


def finish(t, field, modes, q_count, bands, octets, rest, gs, vb, rt, scr):
    blocks = gs.shape[0] // 2
    near = gs.shape[2] // LANES
    span = LANES // bands
    halves = bands * bands // LANES
    quad = 16 // (halves * q_count)
    many = span // quad
    k_count = near * blocks * span
    last = modes // 8 * q_count
    sets = [j * q_count + q for j in octets for q in range(q_count)] + ([last] if rest else [])
    for c in range(2):
        for o in range(near):
            for n in range(len(sets)):
                tiles = []
                for i in range(8):
                    at = (n * 8 + i) * bands
                    tiles.append(field[c][at : at + bands, o * LANES : (o + 1) * LANES])
                for i, tile in enumerate(exchange(tiles, bands)):
                    at = (c * span + i) * bands
                    rt[o, n, at : at + bands, :] = tile
    turn = iota((16, LANES), 0) & (q_count - 1)

    def choose(tiles):
        tile = tiles[0]
        for q in range(1, q_count):
            tile = jnp.where(turn == q, tiles[q], tile)
        return tile

    for o in range(near):
        right = jnp.concatenate([rt[o, n] for n in range(len(sets))], axis=1)
        done = dot(vb[t * near + o], right)
        for c in range(2):
            for g in range(many):
                base = (c * many + g) * span * 16

                def tile(n, i):
                    at = base + i * 16
                    return done[at : at + 16, n * LANES : (n + 1) * LANES].astype(bf16)

                found = []
                for j in range(len(octets)):
                    found += exchange(
                        [choose([tile(j * q_count + q, i) for q in range(q_count)]) for i in range(span)], bands
                    )
                if rest:
                    tiles = exchange([tile(len(sets) - 1, i) for i in range(span)], bands)
                    found += [choose([tiles[q * rest + i] for q in range(q_count)]) for i in range(rest)]
                for m in range(0, len(found), quad):
                    tiles = (found[m : m + quad] + [None] * quad)[:quad]
                    tiles = exchange(tiles, halves * q_count, 0)
                    at = m * halves * q_count
                    tall = min(quad, len(found) - m) * halves * q_count
                    for i in range(quad):
                        k = (t * near + o) * span + g * quad + i
                        scr[c * k_count + k, at : at + tall, :] = tiles[i][:tall]


def gather_kernel(
    lat_count,
    kpt_count,
    modes,
    qp_hbm,
    rpv_hbm,
    rpw_hbm,
    x_hbm,
    rot_hbm,
    rv_hbm,
    rw_hbm,
    kp_hbm,
    u_hbm,
    v_hbm,
    mk_hbm,
    mkq_hbm,
    gath,
    gs,
    vb,
    acc,
    qp,
    rpv,
    rpw,
    x_ref,
    rot_ref,
    rv_ref,
    rw_ref,
    kp_ref,
    u_ref,
    v_ref,
    mk_ref,
    mkq_ref,
    xs,
    wre,
    wim,
    part,
    recv,
    turned,
    p2,
    u2,
    v2,
    loads,
    lat_send,
    lat_recv,
    chip_send,
    chip_recv,
    pair_send,
    pair_recv,
):
    given = (qp_hbm, rpv_hbm, rpw_hbm, x_hbm, rot_hbm, rv_hbm, rw_hbm, kp_hbm, u_hbm, v_hbm, mk_hbm, mkq_hbm)
    held = (qp, rpv, rpw, x_ref, rot_ref, rv_ref, rw_ref, kp_ref, u_ref, v_ref, mk_ref, mkq_ref)
    load = []
    for i in range(len(given)):
        load.append(pltpu.make_async_copy(given[i], held[i], loads.at[i]))
        load[i].start()
    lat = lax.axis_index("lat")
    kpt = lax.axis_index("kpt")
    chips = kpt_count // 2
    chip = kpt // 2
    core = kpt - 2 * chip
    pair = 2 * chip + 1 - core

    def lat_peer(step):
        return lax.rem(lat + step, lat_count)

    def chip_peer(step):
        return lax.rem(chip + step, chips)

    barrier = pltpu.get_barrier_semaphore()
    for step in range(1, lat_count):
        pl.semaphore_signal(barrier, inc=1, device_id=(lat_peer(step), kpt), device_id_type=MESH)
    for step in range(1, chips):
        pl.semaphore_signal(barrier, inc=1, device_id=(lat, 2 * chip_peer(step) + core), device_id_type=MESH)
    pl.semaphore_signal(barrier, inc=1, device_id=(lat, pair), device_id_type=MESH)

    q_count = rot_ref.shape[1]
    mode_count = rot_ref.shape[2]
    local = x_ref.shape[2]
    bands = mk_ref.shape[0]
    k_count = mk_ref.shape[1]
    width = bands * bands
    halves = width // LANES
    cells = rv_ref.shape[1]
    sets = part.shape[0]
    qn = sets * 8
    span = LANES // bands
    quad = 16 // (halves * q_count)

    for copy in load[:5]:
        copy.wait()
    if q_count * modes != qn:
        wre[...] = jnp.zeros_like(wre)
        wim[...] = jnp.zeros_like(wim)
    for q in range(q_count):
        term = qp[q : q + 1, :] * rpv[...].astype(f32)
        argument = two_pi * (term[:, 0:1] + term[:, 1:2] + term[:, 2:3])
        argument = jnp.broadcast_to(argument, (1, mode_count))
        inverse = 1.0 / jnp.broadcast_to(rpw[...].astype(f32), (1, mode_count))
        pr = (jnp.cos(argument) * inverse).astype(bf16).astype(f32)
        pi = (jnp.sin(argument) * inverse).astype(bf16).astype(f32)
        mr = rot_ref[0, q].astype(f32).T
        mi = rot_ref[1, q].astype(f32).T
        wr = pr * mr - pi * mi
        wi = pr * mi + pi * mr
        for d in range(lat_count):
            rest = modes % 8
            for n in range(0, modes, 8):
                take = min(8, modes - n)
                rows = slice(d * modes + n, d * modes + n + take)
                at = d * 2 * qn + (n // 8 * q_count + q) * 16
                if take == rest:
                    at = d * 2 * qn + n // 8 * q_count * 16 + q * rest
                wre[at : at + take, :] = wr[rows]
                wim[at : at + take, :] = -wi[rows]
                wre[at + 8 : at + 8 + take, :] = wi[rows]
                wim[at + 8 : at + 8 + take, :] = wr[rows]

    for c in range(2):
        x = x_ref[c, 0].astype(f32)
        for m in range(mode_count):
            for h in range(halves):
                at = (h * mode_count + m) * 2 * local + c * local
                lane = m * width + h * LANES
                xs[at : at + local, :] = x[:, lane : lane + LANES]

    def rows_of(c, e):
        return jnp.concatenate(
            [
                xs[pl.ds(h * mode_count * 2 * local + c * local + e, mode_count, stride=2 * local), :]
                for h in range(halves)
            ],
            axis=1,
        ).astype(bf16)

    left, right = wre[...].astype(bf16), wim[...].astype(bf16)
    for e in range(local):
        piece = (dot(left, rows_of(0, e)) + dot(right, rows_of(1, e))).astype(bf16)
        for d in range(lat_count):
            for i in range(sets):
                at = d * 2 * qn + i * 16
                part[i, d, e] = piece[at : at + 16]

    pl.semaphore_wait(barrier, lat_count + chips - 1)
    first = [
        [
            pltpu.make_async_remote_copy(
                src_ref=part.at[i, lat_peer(step)],
                dst_ref=recv.at[i, lat],
                send_sem=lat_send.at[i, step],
                recv_sem=lat_recv.at[i, step],
                device_id=(lat_peer(step), kpt),
                device_id_type=MESH,
            )
            for step in range(1, lat_count)
        ]
        for i in range(sets)
    ]
    for copies in first:
        for copy in copies:
            copy.start()

    for copy in load[5:]:
        copy.wait()
    size = bands * k_count
    spread = iota((k_count, size), 1) - bands * iota((k_count, size), 0)
    spread = ((spread >= 0) & (spread < bands)).astype(f32).astype(bf16)
    eye = iota((cells, cells), 0) == iota((cells, cells), 1)

    def column(row):
        return jnp.sum(jnp.where(eye, row, 0.0), axis=1, keepdims=True)

    column_of = [column(rv_ref[i : i + 1, :].astype(f32)) for i in range(3)]
    argument = two_pi * (
        kp_ref[0:1, :] * column_of[0] + kp_ref[1:2, :] * column_of[1] + kp_ref[2:3, :] * column_of[2]
    )
    inverse = 1.0 / column(rw_ref[...].astype(f32))
    p2[0] = dot((jnp.cos(argument) * inverse).astype(bf16), spread)
    p2[1] = dot((jnp.sin(argument) * inverse).astype(bf16), spread)

    row = iota((width, size), 0)
    lane = iota((width, size), 1) & (bands - 1)
    pick = iota((bands, width), 1)
    order = iota((bands, width), 0)
    minor = (row & (bands - 1)) == lane
    major = (row // bands) == lane
    take_major = ((pick // bands) == order).astype(f32).astype(bf16)
    take_minor = ((pick & (bands - 1)) == order).astype(f32).astype(bf16)
    keep = jnp.concatenate([mk_ref[...].astype(f32)] * bands, axis=0)
    for c in range(2):
        wide = dot((u_ref[c].astype(f32) * keep).astype(bf16), spread)
        u2[c] = dot(take_major, jnp.where(minor, wide, 0.0).astype(bf16))
    blocks = gs.shape[0] // 2
    lanes = gs.shape[2]

    def grow(e, carry):
        pr, pi = p2[0, pl.ds(e, 1), :], p2[1, pl.ds(e, 1), :]
        re = (pr * u2[0] - pi * u2[1]).astype(bf16)
        im = pr * u2[1] + pi * u2[0]
        minus = (-im).astype(bf16)
        im = im.astype(bf16)
        at = pl.ds(pl.multiple_of(e * 2 * bands, bands), bands)
        below = pl.ds(pl.multiple_of(e * 2 * bands + bands, bands), bands)
        for t in range(blocks):
            cut = slice(t * lanes, (t + 1) * lanes)
            gs[t, at, :] = re[:, cut]
            gs[blocks + t, at, :] = im[:, cut]
            gs[t, below, :] = minus[:, cut]
            gs[blocks + t, below, :] = re[:, cut]
        return carry

    lax.fori_loop(0, cells, grow, 0)

    tall = 2 * bands * span * q_count

    def lay(stage):
        if stage == 0:
            for q in range(q_count):
                keep = jnp.concatenate([mkq_ref[q].astype(f32)] * bands, axis=0)
                turn = []
                for c in range(2):
                    wide = dot((v_ref[c, q].astype(f32) * keep).astype(bf16), spread)
                    turn.append(dot(take_minor, jnp.where(major, wide, 0.0).astype(bf16)).astype(bf16))
                at = q * 2 * bands
                v2[0, at : at + bands, :], v2[0, at + bands : at + 2 * bands, :] = turn[0], -turn[1]
                v2[1, at : at + bands, :], v2[1, at + bands : at + 2 * bands, :] = turn[1], turn[0]
            return
        row = iota((tall, LANES), 0)
        at_k = ((row // (span * 16)) & (span // quad - 1)) * quad + ((row // (halves * q_count)) & (quad - 1))
        same = at_k == iota((tall, LANES), 1) // bands
        row = iota((tall, q_count * 2 * bands), 0)
        band = ((row // q_count) & (halves - 1)) * span + ((row // 16) & (span - 1))
        band = ((row & (q_count - 1)) * 2 + row // (tall // 2)) * bands + band
        repeat = (band == iota((tall, q_count * 2 * bands), 1)).astype(f32).astype(bf16)
        for o in range(k_count // span):
            for c in range(2):
                wide = dot(repeat, v2[c, :, o * LANES : (o + 1) * LANES])
                vb[o, :, c * LANES : (c + 1) * LANES] = jnp.where(same, wide, 0.0).astype(bf16)

    def over(source, i, target, send_sem, recv_sem):
        return pltpu.make_async_remote_copy(
            src_ref=gath.at[source, i],
            dst_ref=gath.at[source, i],
            send_sem=send_sem,
            recv_sem=recv_sem,
            device_id=(lat, target),
            device_id_type=MESH,
        )

    def outward(i, act):
        for down in (True, False):
            for z in range(chips) if down else reversed(range(chips)):

                @pl.when((chip > z) if down else (chip < z))
                def _():
                    act(over(kpt, i, 2 * z + core, chip_send.at[i, z], chip_recv.at[i, chip]))

    def start(copy):
        copy.start()

    def sent(copy):
        copy.wait_send()

    third = []

    def pass_on(source, i, step):
        copy = over(source, i, pair, pair_send.at[i, step], pair_recv.at[i, step])
        copy.start()
        third.append((copy, step))

    def begin(near):
        for copy, step in third:
            if step in (0, chips - 1):
                copy.wait_recv()
        for t in range(2 * blocks):
            acc[t] = cell_sum(t, [chip, near], gath, gs)

    cut = span // 2
    for i in range(sets):
        for copy in first[i]:
            copy.wait_recv()
        for g in range(local // cut):
            rows = []
            for e in range(g * cut, (g + 1) * cut):
                total = part[i, lat, e].astype(f32)
                for step in range(1, lat_count):
                    total = total + recv[i, lat_peer(step), e].astype(f32)
                rows += [total[:8], total[8:]]
            for h in range(halves):
                tiles = exchange([r[:, h * LANES : (h + 1) * LANES] for r in rows], bands)
                for a in range(span):
                    turned[pl.ds(h * span + a, 8, stride=bands), :] = tiles[a]
            gath[kpt, i, g] = turned[...].astype(bf16)
        outward(i, start)
        pass_on(kpt, i, chips - 1)

    nearest = [apart(chip, chips, step) for step in range(chips - 1)]
    waits = sorted(
        ((i + min(step, 1) + 0.1 * step, step, i) for step in range(chips - 1) for i in range(sets))
    )
    ready = [n for n, (_, step, _) in enumerate(waits) if step == 0][-1] + 2
    stage = 0
    for n, (_, step, i) in enumerate(waits):
        if stage < 2 and n in (1, 3):
            lay(stage)
            stage += 1
        if n == ready:
            begin(nearest[0])
        source = nearest[step]
        over(2 * source + core, i, pair, chip_send.at[i, 0], chip_recv.at[i, source]).wait_recv()
        pass_on(2 * source + core, i, step)
    while stage < 2:
        lay(stage)
        stage += 1
    if ready >= len(waits):
        begin(nearest[0])
    for copy, step in third:
        if 0 < step < chips - 1:
            copy.wait_recv()
    for copies in first:
        for copy in copies:
            copy.wait_send()
    for copy, _ in third:
        copy.wait_send()
    for i in range(sets):
        outward(i, sent)


def couple_kernel(modes, q_count, bands, gath, gs, vb, acc, out_ref, rt, scr, sems):
    blocks = gs.shape[0] // 2
    span = LANES // bands
    near = gs.shape[2] // LANES
    k_count = near * blocks * span
    held = out_ref.shape[1]
    chips = gath.shape[0] // 2
    rest = [apart(lax.axis_index("kpt") // 2, chips, step) for step in range(1, chips - 1)]

    def total(t):
        return tuple(
            (acc[c * blocks + t] + cell_sum(c * blocks + t, rest, gath, gs)).astype(bf16) for c in range(2)
        )

    def leave(t):
        copies = []
        for c in range(2):
            rows = pl.ds(c * k_count + t * near * span, near * span)
            copies.append(pltpu.make_async_copy(scr.at[rows, :held], out_ref.at[rows], sems.at[t, c]))
        return copies

    def step(t, field):
        ahead = total(jnp.minimum(t + 1, blocks - 1))
        finish(t, field, modes, q_count, bands, range(modes // 8), modes % 8, gs, vb, rt, scr)
        for copy in leave(t):
            copy.start()
        return ahead

    lax.fori_loop(0, blocks, step, total(0))
    for t in range(blocks):
        for copy in leave(t):
            copy.wait()


def per_device(
    lat_count,
    kpt_count,
    coarse,
    rp_vectors,
    rp_weights,
    re_vectors,
    re_weights,
    q_points,
    k_points,
    modes_rot,
    u_k,
    u_kq,
    mask_k,
    mask_kq,
):
    q_count = q_points.shape[0]
    k_count = k_points.shape[0]
    bands = u_k.shape[2]
    width = bands * bands
    local = coarse.shape[2]
    mode_count = coarse.shape[3] // width
    modes = mode_count // lat_count
    cells = re_vectors.shape[0]
    span = LANES // bands
    qn = modes // 8 * 8 * q_count + up(modes % 8 * q_count, 8)
    sets = qn // 8
    groups = local // (span // 2)
    octets = -(-modes // span)
    chips = kpt_count // 2
    lanes = 2 * LANES
    blocks = bands * k_count // lanes
    assert chips > 2 and coarse.shape[1] == 1 and local % (span // 2) == 0 and bands & (bands - 1) == 0

    uk = jnp.transpose(u_k, (0, 2, 3, 1)).reshape(2, width, k_count)
    ukq = jnp.transpose(u_kq, (0, 1, 3, 4, 2)).reshape(2, q_count, width, k_count)
    keep_k = jnp.transpose(mask_k)
    keep_kq = jnp.transpose(mask_kq, (0, 2, 1))

    anywhere = pl.BlockSpec(memory_space=pltpu.HBM)
    vmem = pl.BlockSpec(memory_space=pltpu.VMEM)
    dma = pltpu.SemaphoreType.DMA
    tall = span * q_count * 2 * bands
    inputs = (
        q_points,
        rp_vectors,
        rp_weights.reshape(1, 1),
        coarse,
        modes_rot,
        jnp.transpose(re_vectors),
        re_weights.reshape(1, cells),
        jnp.transpose(k_points),
        uk,
        ukq,
        keep_k,
        keep_kq,
    )
    count = modes * (width // LANES)
    held = count * q_count
    shapes = [
        ((kpt_count, sets, groups, 8 * bands, LANES), bf16),
        ((2 * blocks, 2 * cells * bands, lanes), bf16),
        ((k_count // span, tall, 2 * LANES), bf16),
        ((2 * blocks, qn * bands, lanes), f32),
    ]
    kept = sum(4 * math.prod(shape) for shape, _ in shapes[3:]) + sum(2 * math.prod(shape) for shape, _ in shapes[:3])
    parts = pl.pallas_call(
        functools.partial(gather_kernel, lat_count, kpt_count, modes),
        in_specs=[anywhere] * len(inputs),
        out_specs=[vmem] * len(shapes),
        out_shape=[pltpu.VMEM(shape, dtype) for shape, dtype in shapes],
        scratch_shapes=[pltpu.VMEM(x.shape, x.dtype) for x in inputs]
        + [
            pltpu.VMEM((2 * local * mode_count * (width // LANES), LANES), f32),
            pltpu.VMEM((lat_count * 2 * qn, mode_count), f32),
            pltpu.VMEM((lat_count * 2 * qn, mode_count), f32),
            pltpu.VMEM((sets, lat_count, local, 16, width), bf16),
            pltpu.VMEM((sets, lat_count, local, 16, width), bf16),
            pltpu.VMEM((8 * bands, LANES), f32),
            pltpu.VMEM((2, cells, bands * k_count), f32),
            pltpu.VMEM((2, bands, bands * k_count), f32),
            pltpu.VMEM((2, q_count * 2 * bands, bands * k_count), bf16),
            dma((len(inputs),)),
            dma((sets, lat_count)),
            dma((sets, lat_count)),
            dma((sets, chips)),
            dma((sets, chips)),
            dma((sets, chips)),
            dma((sets, chips)),
        ],
        compiler_params=pltpu.CompilerParams(
            collective_id=0, has_side_effects=True, vmem_limit_bytes=63 * 1024 * 1024 - kept
        ),
    )(*inputs)
    result = jax.ShapeDtypeStruct((2 * k_count, held, LANES), bf16)
    out = pl.pallas_call(
        functools.partial(couple_kernel, modes, q_count, bands),
        in_specs=[vmem] * len(parts),
        out_specs=anywhere,
        out_shape=result,
        scratch_shapes=[
            pltpu.VMEM((lanes // LANES, sets, 2 * LANES, LANES), bf16),
            pltpu.VMEM((2 * k_count, up(held, 16), LANES), bf16),
            dma((blocks, 2)),
        ],
        compiler_params=pltpu.CompilerParams(vmem_limit_bytes=40 * 1024 * 1024),
    )(*parts)
    out = out.reshape(2, k_count, count, q_count, LANES)
    return jnp.transpose(out, (0, 1, 3, 2, 4)).reshape(2, k_count, q_count, modes * width)


def solution(mesh):
    placed = (
        P(None, "lat", "kpt", None),
        P("lat", None),
        P("lat"),
        P(),
        P(),
        P(),
        P("kpt", None),
        P(),
        P(None, "kpt", None, None),
        P(None, None, "kpt", None, None),
        P("kpt", None),
        P(None, "kpt", None),
    )
    return jax.shard_map(
        functools.partial(per_device, mesh.shape["lat"], mesh.shape["kpt"]),
        mesh=mesh,
        in_specs=placed,
        out_specs=P(None, "kpt", None, "lat"),
        check_vma=False,
    )
```

```python
import functools
import math

import jax
import jax.numpy as jnp
from jax import lax
from jax.experimental import pallas as pl
from jax.experimental.pallas import tpu as pltpu
from jax.sharding import PartitionSpec as P

two_pi = 6.283185307179586
f32 = jnp.float32
bf16 = jnp.bfloat16
i32 = jnp.int32
MESH = pl.DeviceIdType.MESH
LANES = 128


def up(value, step):
    return -(-value // step) * step


def iota(shape, axis):
    return lax.broadcasted_iota(i32, shape, axis)


def dot(a, b):
    return jnp.dot(a, b, preferred_element_type=f32)


def exchange(tiles, unit, axis=1):
    span = len(tiles)
    shape = next(t for t in tiles if t is not None).shape
    place = iota(shape, axis)
    skew = [t if i == 0 or t is None else pltpu.roll(t, i * unit, axis) for i, t in enumerate(tiles)]
    tiles = [skew[-i % span] for i in range(span)]
    bit = 1
    while bit < span:
        odd = (place & (unit * bit)) != 0
        turned = []
        for i in range(span):
            a, b = tiles[i], tiles[(i - bit) % span]
            turned.append(b if a is None else a if b is None else jnp.where(odd, b, a))
        tiles = turned
        bit *= 2
    return [t if i == 0 else pltpu.roll(t, shape[axis] - i * unit, axis) for i, t in enumerate(tiles)]


def apart(chip, chips, step):
    found = 0
    for z in range(chips):
        others = sorted((o for o in range(chips) if o != z), key=lambda o: abs(o - z))
        found = found + jnp.where(chip == z, others[step], 0)
    return found


def cell_sum(t, some, gath, gs):
    _, sets, groups = gath.shape[:3]
    deep = 2 * groups * LANES
    left = jnp.concatenate(
        [
            jnp.concatenate([gath[2 * z + c, i, g] for z in some for c in range(2) for g in range(groups)], axis=1)
            for i in range(sets)
        ],
        axis=0,
    )
    right = [gs[t, pl.ds(pl.multiple_of(z * deep, deep), deep), :] for z in some]
    return dot(left, jnp.concatenate(right, axis=0))


def finish(t, field, modes, q_count, bands, octets, rest, gs, vb, rt, scr):
    blocks = gs.shape[0] // 2
    near = gs.shape[2] // LANES
    span = LANES // bands
    halves = bands * bands // LANES
    quad = 16 // (halves * q_count)
    many = span // quad
    k_count = near * blocks * span
    last = modes // 8 * q_count
    sets = [j * q_count + q for j in octets for q in range(q_count)] + ([last] if rest else [])
    for c in range(2):
        for o in range(near):
            for n in range(len(sets)):
                tiles = []
                for i in range(8):
                    at = (n * 8 + i) * bands
                    tiles.append(field[c][at : at + bands, o * LANES : (o + 1) * LANES])
                for i, tile in enumerate(exchange(tiles, bands)):
                    at = (c * span + i) * bands
                    rt[o, n, at : at + bands, :] = tile
    turn = iota((16, LANES), 0) & (q_count - 1)

    def choose(tiles):
        tile = tiles[0]
        for q in range(1, q_count):
            tile = jnp.where(turn == q, tiles[q], tile)
        return tile

    for o in range(near):
        right = jnp.concatenate([rt[o, n] for n in range(len(sets))], axis=1)
        done = dot(vb[t * near + o], right)
        for c in range(2):
            for g in range(many):
                base = (c * many + g) * span * 16

                def tile(n, i):
                    at = base + i * 16
                    return done[at : at + 16, n * LANES : (n + 1) * LANES].astype(bf16)

                found = []
                for j in range(len(octets)):
                    found += exchange(
                        [choose([tile(j * q_count + q, i) for q in range(q_count)]) for i in range(span)], bands
                    )
                if rest:
                    tiles = exchange([tile(len(sets) - 1, i) for i in range(span)], bands)
                    found += [choose([tiles[q * rest + i] for q in range(q_count)]) for i in range(rest)]
                for m in range(0, len(found), quad):
                    tiles = (found[m : m + quad] + [None] * quad)[:quad]
                    tiles = exchange(tiles, halves * q_count, 0)
                    at = m * halves * q_count
                    tall = min(quad, len(found) - m) * halves * q_count
                    for i in range(quad):
                        k = (t * near + o) * span + g * quad + i
                        scr[c * k_count + k, at : at + tall, :] = tiles[i][:tall]


def gather_kernel(
    lat_count,
    kpt_count,
    modes,
    qp_hbm,
    rpv_hbm,
    rpw_hbm,
    x_hbm,
    rot_hbm,
    rv_hbm,
    rw_hbm,
    kp_hbm,
    u_hbm,
    v_hbm,
    mk_hbm,
    mkq_hbm,
    gath,
    gs,
    vb,
    acc,
    qp,
    rpv,
    rpw,
    x_ref,
    rot_ref,
    rv_ref,
    rw_ref,
    kp_ref,
    u_ref,
    v_ref,
    mk_ref,
    mkq_ref,
    xs,
    wre,
    wim,
    part,
    recv,
    turned,
    p2,
    u2,
    v2,
    loads,
    lat_send,
    lat_recv,
    chip_send,
    chip_recv,
    pair_send,
    pair_recv,
):
    given = (qp_hbm, rpv_hbm, rpw_hbm, x_hbm, rot_hbm, rv_hbm, rw_hbm, kp_hbm, u_hbm, v_hbm, mk_hbm, mkq_hbm)
    held = (qp, rpv, rpw, x_ref, rot_ref, rv_ref, rw_ref, kp_ref, u_ref, v_ref, mk_ref, mkq_ref)
    load = []
    for i in range(len(given)):
        load.append(pltpu.make_async_copy(given[i], held[i], loads.at[i]))
        load[i].start()
    lat = lax.axis_index("lat")
    kpt = lax.axis_index("kpt")
    chips = kpt_count // 2
    chip = kpt // 2
    core = kpt - 2 * chip
    pair = 2 * chip + 1 - core

    def lat_peer(step):
        return lax.rem(lat + step, lat_count)

    def chip_peer(step):
        return lax.rem(chip + step, chips)

    barrier = pltpu.get_barrier_semaphore()
    for step in range(1, lat_count):
        pl.semaphore_signal(barrier, inc=1, device_id=(lat_peer(step), kpt), device_id_type=MESH)
    for step in range(1, chips):
        pl.semaphore_signal(barrier, inc=1, device_id=(lat, 2 * chip_peer(step) + core), device_id_type=MESH)
    pl.semaphore_signal(barrier, inc=1, device_id=(lat, pair), device_id_type=MESH)

    q_count = rot_ref.shape[1]
    mode_count = rot_ref.shape[2]
    local = x_ref.shape[2]
    bands = mk_ref.shape[0]
    k_count = mk_ref.shape[1]
    width = bands * bands
    halves = width // LANES
    cells = rv_ref.shape[1]
    sets = part.shape[0]
    qn = sets * 8
    span = LANES // bands
    quad = 16 // (halves * q_count)

    for copy in load[:5]:
        copy.wait()
    if q_count * modes != qn:
        wre[...] = jnp.zeros_like(wre)
        wim[...] = jnp.zeros_like(wim)
    for q in range(q_count):
        term = qp[q : q + 1, :] * rpv[...].astype(f32)
        argument = two_pi * (term[:, 0:1] + term[:, 1:2] + term[:, 2:3])
        argument = jnp.broadcast_to(argument, (1, mode_count))
        inverse = 1.0 / jnp.broadcast_to(rpw[...].astype(f32), (1, mode_count))
        pr = (jnp.cos(argument) * inverse).astype(bf16).astype(f32)
        pi = (jnp.sin(argument) * inverse).astype(bf16).astype(f32)
        mr = rot_ref[0, q].astype(f32).T
        mi = rot_ref[1, q].astype(f32).T
        wr = pr * mr - pi * mi
        wi = pr * mi + pi * mr
        for d in range(lat_count):
            rest = modes % 8
            for n in range(0, modes, 8):
                take = min(8, modes - n)
                rows = slice(d * modes + n, d * modes + n + take)
                at = d * 2 * qn + (n // 8 * q_count + q) * 16
                if take == rest:
                    at = d * 2 * qn + n // 8 * q_count * 16 + q * rest
                wre[at : at + take, :] = wr[rows]
                wim[at : at + take, :] = -wi[rows]
                wre[at + 8 : at + 8 + take, :] = wi[rows]
                wim[at + 8 : at + 8 + take, :] = wr[rows]

    for c in range(2):
        x = x_ref[c, 0].astype(f32)
        for m in range(mode_count):
            for h in range(halves):
                at = (h * mode_count + m) * 2 * local + c * local
                lane = m * width + h * LANES
                xs[at : at + local, :] = x[:, lane : lane + LANES]

    def rows_of(c, e):
        return jnp.concatenate(
            [
                xs[pl.ds(h * mode_count * 2 * local + c * local + e, mode_count, stride=2 * local), :]
                for h in range(halves)
            ],
            axis=1,
        ).astype(bf16)

    left, right = wre[...].astype(bf16), wim[...].astype(bf16)
    for e in range(local):
        piece = (dot(left, rows_of(0, e)) + dot(right, rows_of(1, e))).astype(bf16)
        for d in range(lat_count):
            for i in range(sets):
                at = d * 2 * qn + i * 16
                part[i, d, e] = piece[at : at + 16]

    pl.semaphore_wait(barrier, lat_count + chips - 1)
    first = [
        [
            pltpu.make_async_remote_copy(
                src_ref=part.at[i, lat_peer(step)],
                dst_ref=recv.at[i, lat],
                send_sem=lat_send.at[i, step],
                recv_sem=lat_recv.at[i, step],
                device_id=(lat_peer(step), kpt),
                device_id_type=MESH,
            )
            for step in range(1, lat_count)
        ]
        for i in range(sets)
    ]
    for copies in first:
        for copy in copies:
            copy.start()

    for copy in load[5:]:
        copy.wait()
    size = bands * k_count
    spread = iota((k_count, size), 1) - bands * iota((k_count, size), 0)
    spread = ((spread >= 0) & (spread < bands)).astype(f32).astype(bf16)
    eye = iota((cells, cells), 0) == iota((cells, cells), 1)

    def column(row):
        return jnp.sum(jnp.where(eye, row, 0.0), axis=1, keepdims=True)

    column_of = [column(rv_ref[i : i + 1, :].astype(f32)) for i in range(3)]
    argument = two_pi * (
        kp_ref[0:1, :] * column_of[0] + kp_ref[1:2, :] * column_of[1] + kp_ref[2:3, :] * column_of[2]
    )
    inverse = 1.0 / column(rw_ref[...].astype(f32))
    p2[0] = dot((jnp.cos(argument) * inverse).astype(bf16), spread)
    p2[1] = dot((jnp.sin(argument) * inverse).astype(bf16), spread)

    row = iota((width, size), 0)
    lane = iota((width, size), 1) & (bands - 1)
    pick = iota((bands, width), 1)
    order = iota((bands, width), 0)
    minor = (row & (bands - 1)) == lane
    major = (row // bands) == lane
    take_major = ((pick // bands) == order).astype(f32).astype(bf16)
    take_minor = ((pick & (bands - 1)) == order).astype(f32).astype(bf16)
    keep = jnp.concatenate([mk_ref[...].astype(f32)] * bands, axis=0)
    for c in range(2):
        wide = dot((u_ref[c].astype(f32) * keep).astype(bf16), spread)
        u2[c] = dot(take_major, jnp.where(minor, wide, 0.0).astype(bf16))
    blocks = gs.shape[0] // 2
    lanes = gs.shape[2]

    def grow(e, carry):
        pr, pi = p2[0, pl.ds(e, 1), :], p2[1, pl.ds(e, 1), :]
        re = (pr * u2[0] - pi * u2[1]).astype(bf16)
        im = pr * u2[1] + pi * u2[0]
        minus = (-im).astype(bf16)
        im = im.astype(bf16)
        at = pl.ds(pl.multiple_of(e * 2 * bands, bands), bands)
        below = pl.ds(pl.multiple_of(e * 2 * bands + bands, bands), bands)
        for t in range(blocks):
            cut = slice(t * lanes, (t + 1) * lanes)
            gs[t, at, :] = re[:, cut]
            gs[blocks + t, at, :] = im[:, cut]
            gs[t, below, :] = minus[:, cut]
            gs[blocks + t, below, :] = re[:, cut]
        return carry

    lax.fori_loop(0, cells, grow, 0)

    tall = 2 * bands * span * q_count

    def lay(stage):
        if stage == 0:
            for q in range(q_count):
                keep = jnp.concatenate([mkq_ref[q].astype(f32)] * bands, axis=0)
                turn = []
                for c in range(2):
                    wide = dot((v_ref[c, q].astype(f32) * keep).astype(bf16), spread)
                    turn.append(dot(take_minor, jnp.where(major, wide, 0.0).astype(bf16)).astype(bf16))
                at = q * 2 * bands
                v2[0, at : at + bands, :], v2[0, at + bands : at + 2 * bands, :] = turn[0], -turn[1]
                v2[1, at : at + bands, :], v2[1, at + bands : at + 2 * bands, :] = turn[1], turn[0]
            return
        row = iota((tall, LANES), 0)
        at_k = ((row // (span * 16)) & (span // quad - 1)) * quad + ((row // (halves * q_count)) & (quad - 1))
        same = at_k == iota((tall, LANES), 1) // bands
        row = iota((tall, q_count * 2 * bands), 0)
        band = ((row // q_count) & (halves - 1)) * span + ((row // 16) & (span - 1))
        band = ((row & (q_count - 1)) * 2 + row // (tall // 2)) * bands + band
        repeat = (band == iota((tall, q_count * 2 * bands), 1)).astype(f32).astype(bf16)
        for o in range(k_count // span):
            for c in range(2):
                wide = dot(repeat, v2[c, :, o * LANES : (o + 1) * LANES])
                vb[o, :, c * LANES : (c + 1) * LANES] = jnp.where(same, wide, 0.0).astype(bf16)

    def over(source, i, target, send_sem, recv_sem):
        return pltpu.make_async_remote_copy(
            src_ref=gath.at[source, i],
            dst_ref=gath.at[source, i],
            send_sem=send_sem,
            recv_sem=recv_sem,
            device_id=(lat, target),
            device_id_type=MESH,
        )

    def outward(i, act):
        for down in (True, False):
            for z in range(chips) if down else reversed(range(chips)):

                @pl.when((chip > z) if down else (chip < z))
                def _():
                    act(over(kpt, i, 2 * z + core, chip_send.at[i, z], chip_recv.at[i, chip]))

    def start(copy):
        copy.start()

    def sent(copy):
        copy.wait_send()

    third = []

    def pass_on(source, i, step):
        copy = over(source, i, pair, pair_send.at[i, step], pair_recv.at[i, step])
        copy.start()
        third.append((copy, step))

    def begin(near):
        for copy, step in third:
            if step in (0, chips - 1):
                copy.wait_recv()
        for t in range(2 * blocks):
            acc[t] = cell_sum(t, [chip, near], gath, gs)

    cut = span // 2
    for i in range(sets):
        for copy in first[i]:
            copy.wait_recv()
        for g in range(local // cut):
            rows = []
            for e in range(g * cut, (g + 1) * cut):
                total = part[i, lat, e].astype(f32)
                for step in range(1, lat_count):
                    total = total + recv[i, lat_peer(step), e].astype(f32)
                rows += [total[:8], total[8:]]
            for h in range(halves):
                tiles = exchange([r[:, h * LANES : (h + 1) * LANES] for r in rows], bands)
                for a in range(span):
                    turned[pl.ds(h * span + a, 8, stride=bands), :] = tiles[a]
            gath[kpt, i, g] = turned[...].astype(bf16)
        outward(i, start)
        pass_on(kpt, i, chips - 1)

    nearest = [apart(chip, chips, step) for step in range(chips - 1)]
    waits = sorted(
        ((i + min(step, 1) + 0.1 * step, step, i) for step in range(chips - 1) for i in range(sets))
    )
    ready = [n for n, (_, step, _) in enumerate(waits) if step == 0][-1] + 2
    stage = 0
    for n, (_, step, i) in enumerate(waits):
        if stage < 2 and n in (1, 3):
            lay(stage)
            stage += 1
        if n == ready:
            begin(nearest[0])
        source = nearest[step]
        over(2 * source + core, i, pair, chip_send.at[i, 0], chip_recv.at[i, source]).wait_recv()
        pass_on(2 * source + core, i, step)
    while stage < 2:
        lay(stage)
        stage += 1
    if ready >= len(waits):
        begin(nearest[0])
    for copy, step in third:
        if 0 < step < chips - 1:
            copy.wait_recv()
    for copies in first:
        for copy in copies:
            copy.wait_send()
    for copy, _ in third:
        copy.wait_send()
    for i in range(sets):
        outward(i, sent)


def couple_kernel(modes, q_count, bands, gath, gs, vb, acc, out_ref, rt, scr, sems):
    blocks = gs.shape[0] // 2
    span = LANES // bands
    near = gs.shape[2] // LANES
    k_count = near * blocks * span
    held = out_ref.shape[1]
    chips = gath.shape[0] // 2
    rest = [apart(lax.axis_index("kpt") // 2, chips, step) for step in range(1, chips - 1)]

    def total(t):
        return tuple(
            (acc[c * blocks + t] + cell_sum(c * blocks + t, rest, gath, gs)).astype(bf16) for c in range(2)
        )

    def leave(t):
        copies = []
        for c in range(2):
            rows = pl.ds(c * k_count + t * near * span, near * span)
            copies.append(pltpu.make_async_copy(scr.at[rows, :held], out_ref.at[rows], sems.at[t, c]))
        return copies

    def step(t, field):
        ahead = total(t + 1) if t + 1 < blocks else None
        finish(t, field, modes, q_count, bands, range(modes // 8), modes % 8, gs, vb, rt, scr)
        for copy in leave(t):
            copy.start()
        return ahead

    field = total(0)
    for t in range(blocks):
        field = step(t, field)
    for t in range(blocks):
        for copy in leave(t):
            copy.wait()


def per_device(
    lat_count,
    kpt_count,
    coarse,
    rp_vectors,
    rp_weights,
    re_vectors,
    re_weights,
    q_points,
    k_points,
    modes_rot,
    u_k,
    u_kq,
    mask_k,
    mask_kq,
):
    q_count = q_points.shape[0]
    k_count = k_points.shape[0]
    bands = u_k.shape[2]
    width = bands * bands
    local = coarse.shape[2]
    mode_count = coarse.shape[3] // width
    modes = mode_count // lat_count
    cells = re_vectors.shape[0]
    span = LANES // bands
    qn = modes // 8 * 8 * q_count + up(modes % 8 * q_count, 8)
    sets = qn // 8
    groups = local // (span // 2)
    octets = -(-modes // span)
    chips = kpt_count // 2
    lanes = 2 * LANES
    blocks = bands * k_count // lanes
    assert chips > 2 and coarse.shape[1] == 1 and local % (span // 2) == 0 and bands & (bands - 1) == 0

    uk = jnp.transpose(u_k, (0, 2, 3, 1)).reshape(2, width, k_count)
    ukq = jnp.transpose(u_kq, (0, 1, 3, 4, 2)).reshape(2, q_count, width, k_count)
    keep_k = jnp.transpose(mask_k)
    keep_kq = jnp.transpose(mask_kq, (0, 2, 1))

    anywhere = pl.BlockSpec(memory_space=pltpu.HBM)
    vmem = pl.BlockSpec(memory_space=pltpu.VMEM)
    dma = pltpu.SemaphoreType.DMA
    tall = span * q_count * 2 * bands
    inputs = (
        q_points,
        rp_vectors,
        rp_weights.reshape(1, 1),
        coarse,
        modes_rot,
        jnp.transpose(re_vectors),
        re_weights.reshape(1, cells),
        jnp.transpose(k_points),
        uk,
        ukq,
        keep_k,
        keep_kq,
    )
    count = modes * (width // LANES)
    held = count * q_count
    shapes = [
        ((kpt_count, sets, groups, 8 * bands, LANES), bf16),
        ((2 * blocks, 2 * cells * bands, lanes), bf16),
        ((k_count // span, tall, 2 * LANES), bf16),
        ((2 * blocks, qn * bands, lanes), f32),
    ]
    kept = sum(4 * math.prod(shape) for shape, _ in shapes[3:]) + sum(2 * math.prod(shape) for shape, _ in shapes[:3])
    parts = pl.pallas_call(
        functools.partial(gather_kernel, lat_count, kpt_count, modes),
        in_specs=[anywhere] * len(inputs),
        out_specs=[vmem] * len(shapes),
        out_shape=[pltpu.VMEM(shape, dtype) for shape, dtype in shapes],
        scratch_shapes=[pltpu.VMEM(x.shape, x.dtype) for x in inputs]
        + [
            pltpu.VMEM((2 * local * mode_count * (width // LANES), LANES), f32),
            pltpu.VMEM((lat_count * 2 * qn, mode_count), f32),
            pltpu.VMEM((lat_count * 2 * qn, mode_count), f32),
            pltpu.VMEM((sets, lat_count, local, 16, width), bf16),
            pltpu.VMEM((sets, lat_count, local, 16, width), bf16),
            pltpu.VMEM((8 * bands, LANES), f32),
            pltpu.VMEM((2, cells, bands * k_count), f32),
            pltpu.VMEM((2, bands, bands * k_count), f32),
            pltpu.VMEM((2, q_count * 2 * bands, bands * k_count), bf16),
            dma((len(inputs),)),
            dma((sets, lat_count)),
            dma((sets, lat_count)),
            dma((sets, chips)),
            dma((sets, chips)),
            dma((sets, chips)),
            dma((sets, chips)),
        ],
        compiler_params=pltpu.CompilerParams(
            collective_id=0, has_side_effects=True, vmem_limit_bytes=63 * 1024 * 1024 - kept
        ),
    )(*inputs)
    result = jax.ShapeDtypeStruct((2 * k_count, held, LANES), bf16)
    out = pl.pallas_call(
        functools.partial(couple_kernel, modes, q_count, bands),
        in_specs=[vmem] * len(parts),
        out_specs=anywhere,
        out_shape=result,
        scratch_shapes=[
            pltpu.VMEM((lanes // LANES, sets, 2 * LANES, LANES), bf16),
            pltpu.VMEM((2 * k_count, up(held, 16), LANES), bf16),
            dma((blocks, 2)),
        ],
        compiler_params=pltpu.CompilerParams(vmem_limit_bytes=40 * 1024 * 1024),
    )(*parts)
    out = out.reshape(2, k_count, count, q_count, LANES)
    return jnp.transpose(out, (0, 1, 3, 2, 4)).reshape(2, k_count, q_count, modes * width)


def solution(mesh):
    placed = (
        P(None, "lat", "kpt", None),
        P("lat", None),
        P("lat"),
        P(),
        P(),
        P(),
        P("kpt", None),
        P(),
        P(None, "kpt", None, None),
        P(None, None, "kpt", None, None),
        P("kpt", None),
        P(None, "kpt", None),
    )
    return jax.shard_map(
        functools.partial(per_device, mesh.shape["lat"], mesh.shape["kpt"]),
        mesh=mesh,
        in_specs=placed,
        out_specs=P(None, "kpt", None, "lat"),
        check_vma=False,
    )
```

```python
import functools
import math

import jax
import jax.numpy as jnp
from jax import lax
from jax.experimental import pallas as pl
from jax.experimental.pallas import tpu as pltpu
from jax.sharding import PartitionSpec as P

two_pi = 6.283185307179586
f32 = jnp.float32
bf16 = jnp.bfloat16
i32 = jnp.int32
MESH = pl.DeviceIdType.MESH
LANES = 128


def up(value, step):
    return -(-value // step) * step


def iota(shape, axis):
    return lax.broadcasted_iota(i32, shape, axis)


def dot(a, b):
    return jnp.dot(a, b, preferred_element_type=f32)


def exchange(tiles, unit, axis=1):
    span = len(tiles)
    shape = next(t for t in tiles if t is not None).shape
    place = iota(shape, axis)
    skew = [t if i == 0 or t is None else pltpu.roll(t, i * unit, axis) for i, t in enumerate(tiles)]
    tiles = [skew[-i % span] for i in range(span)]
    bit = 1
    while bit < span:
        odd = (place & (unit * bit)) != 0
        turned = []
        for i in range(span):
            a, b = tiles[i], tiles[(i - bit) % span]
            turned.append(b if a is None else a if b is None else jnp.where(odd, b, a))
        tiles = turned
        bit *= 2
    return [t if i == 0 else pltpu.roll(t, shape[axis] - i * unit, axis) for i, t in enumerate(tiles)]


def apart(chip, chips, step):
    found = 0
    for z in range(chips):
        others = sorted((o for o in range(chips) if o != z), key=lambda o: abs(o - z))
        found = found + jnp.where(chip == z, others[step], 0)
    return found


def cell_sum(t, some, gath, gs):
    _, sets, groups = gath.shape[:3]
    deep = groups * LANES
    left = jnp.concatenate(
        [
            jnp.concatenate([gath[j, i, g] for j in some for g in range(groups)], axis=1)
            for i in range(sets)
        ],
        axis=0,
    )
    right = [gs[t, pl.ds(pl.multiple_of(j * deep, deep), deep), :] for j in some]
    return dot(left, jnp.concatenate(right, axis=0))


def finish(t, field, modes, q_count, bands, octets, rest, gs, vb, rt, scr, leave):
    blocks = gs.shape[0] // 2
    near = gs.shape[2] // LANES
    span = LANES // bands
    halves = bands * bands // LANES
    quad = 16 // (halves * q_count)
    many = span // quad
    k_count = near * blocks * span
    last = modes // 8 * q_count
    sets = [j * q_count + q for j in octets for q in range(q_count)] + ([last] if rest else [])
    for c in range(2):
        for o in range(near):
            for n in range(len(sets)):
                tiles = []
                for i in range(8):
                    at = (n * 8 + i) * bands
                    tiles.append(field[c][at : at + bands, o * LANES : (o + 1) * LANES])
                for i, tile in enumerate(exchange(tiles, bands)):
                    at = (c * span + i) * bands
                    rt[o, n, at : at + bands, :] = tile
    turn = iota((16, LANES), 0) & (q_count - 1)

    def choose(tiles):
        tile = tiles[0]
        for q in range(1, q_count):
            tile = jnp.where(turn == q, tiles[q], tile)
        return tile

    for o in range(near):
        right = jnp.concatenate([rt[o, n] for n in range(len(sets))], axis=1)
        done = dot(vb[t * near + o], right)
        for c in range(2):
            for g in range(many):
                base = (c * many + g) * span * 16

                def tile(n, i):
                    at = base + i * 16
                    return done[at : at + 16, n * LANES : (n + 1) * LANES].astype(bf16)

                found = []
                for j in range(len(octets)):
                    found += exchange(
                        [choose([tile(j * q_count + q, i) for q in range(q_count)]) for i in range(span)], bands
                    )
                if rest:
                    tiles = exchange([tile(len(sets) - 1, i) for i in range(span)], bands)
                    found += [choose([tiles[q * rest + i] for q in range(q_count)]) for i in range(rest)]
                for m in range(0, len(found), quad):
                    tiles = (found[m : m + quad] + [None] * quad)[:quad]
                    tiles = exchange(tiles, halves * q_count, 0)
                    at = m * halves * q_count
                    tall = min(quad, len(found) - m) * halves * q_count
                    for i in range(quad):
                        k = (t * near + o) * span + g * quad + i
                        scr[c * k_count + k, at : at + tall, :] = tiles[i][:tall]
        for copy in leave(t * near + o):
            copy.start()


def gather_kernel(
    lat_count,
    kpt_count,
    modes,
    qp_hbm,
    rpv_hbm,
    rpw_hbm,
    x_hbm,
    rot_hbm,
    rv_hbm,
    rw_hbm,
    kp_hbm,
    u_hbm,
    v_hbm,
    mk_hbm,
    mkq_hbm,
    gath,
    gs,
    vb,
    acc,
    qp,
    rpv,
    rpw,
    x_ref,
    rot_ref,
    rv_ref,
    rw_ref,
    kp_ref,
    u_ref,
    v_ref,
    mk_ref,
    mkq_ref,
    xs,
    wre,
    wim,
    part,
    recv,
    turned,
    p2,
    u2,
    v2,
    loads,
    lat_send,
    lat_recv,
    chip_send,
    chip_recv,
    pair_send,
    pair_recv,
):
    given = (qp_hbm, rpv_hbm, rpw_hbm, x_hbm, rot_hbm, rv_hbm, rw_hbm, kp_hbm, u_hbm, v_hbm, mk_hbm, mkq_hbm)
    held = (qp, rpv, rpw, x_ref, rot_ref, rv_ref, rw_ref, kp_ref, u_ref, v_ref, mk_ref, mkq_ref)
    load = []
    for i in range(len(given)):
        load.append(pltpu.make_async_copy(given[i], held[i], loads.at[i]))
    for i in (3, 4, 0, 1, 2, *range(5, len(given))):
        load[i].start()
    lat = lax.axis_index("lat")
    kpt = lax.axis_index("kpt")
    chips = kpt_count // 2
    chip = kpt // 2
    core = kpt - 2 * chip
    pair = 2 * chip + 1 - core

    def lat_peer(step):
        return lax.rem(lat + step, lat_count)

    def chip_peer(step):
        return lax.rem(chip + step, chips)

    barrier = pltpu.get_barrier_semaphore()
    for step in range(1, lat_count):
        pl.semaphore_signal(barrier, inc=1, device_id=(lat_peer(step), kpt), device_id_type=MESH)
    for step in range(1, chips):
        pl.semaphore_signal(barrier, inc=1, device_id=(lat, 2 * chip_peer(step) + core), device_id_type=MESH)
    pl.semaphore_signal(barrier, inc=1, device_id=(lat, pair), device_id_type=MESH)

    q_count = rot_ref.shape[1]
    mode_count = rot_ref.shape[2]
    local = x_ref.shape[2]
    bands = mk_ref.shape[0]
    k_count = mk_ref.shape[1]
    width = bands * bands
    halves = width // LANES
    cells = rv_ref.shape[1]
    sets = part.shape[0]
    qn = sets * 8
    span = LANES // bands
    quad = 16 // (halves * q_count)

    for copy in load[:5]:
        copy.wait()
    if q_count * modes != qn:
        wre[...] = jnp.zeros_like(wre)
        wim[...] = jnp.zeros_like(wim)
    for q in range(q_count):
        term = qp[q : q + 1, :] * rpv[...].astype(f32)
        argument = two_pi * (term[:, 0:1] + term[:, 1:2] + term[:, 2:3])
        argument = jnp.broadcast_to(argument, (1, mode_count))
        inverse = 1.0 / jnp.broadcast_to(rpw[...].astype(f32), (1, mode_count))
        pr = (jnp.cos(argument) * inverse).astype(bf16).astype(f32)
        pi = (jnp.sin(argument) * inverse).astype(bf16).astype(f32)
        mr = rot_ref[0, q].astype(f32).T
        mi = rot_ref[1, q].astype(f32).T
        wr = pr * mr - pi * mi
        wi = pr * mi + pi * mr
        for d in range(lat_count):
            rest = modes % 8
            for n in range(0, modes, 8):
                take = min(8, modes - n)
                rows = slice(d * modes + n, d * modes + n + take)
                at = ((n // 8 * q_count + q) * lat_count + d) * 16
                if take == rest:
                    at = (n // 8 * q_count * lat_count + d) * 16 + q * rest
                wre[at : at + take, :] = wr[rows]
                wim[at : at + take, :] = -wi[rows]
                wre[at + 8 : at + 8 + take, :] = wi[rows]
                wim[at + 8 : at + 8 + take, :] = wr[rows]

    for c in range(2):
        x = x_ref[c, 0].astype(f32)
        for m in range(mode_count):
            for h in range(halves):
                at = (h * mode_count + m) * 2 * local + c * local
                lane = m * width + h * LANES
                xs[at : at + local, :] = x[:, lane : lane + LANES]

    def rows_of(c, e):
        return jnp.concatenate(
            [
                xs[pl.ds(h * mode_count * 2 * local + c * local + e, mode_count, stride=2 * local), :]
                for h in range(halves)
            ],
            axis=1,
        ).astype(bf16)

    first = [
        [
            pltpu.make_async_remote_copy(
                src_ref=part.at[i, lat_peer(step)],
                dst_ref=recv.at[i, lat],
                send_sem=lat_send.at[i, step],
                recv_sem=lat_recv.at[i, step],
                device_id=(lat_peer(step), kpt),
                device_id_type=MESH,
            )
            for step in range(1, lat_count)
        ]
        for i in range(sets)
    ]
    field = [[rows_of(c, e) for e in range(local)] for c in range(2)]
    for i in range(sets):
        cut = slice(i * lat_count * 16, (i + 1) * lat_count * 16)
        left, right = wre[cut, :].astype(bf16), wim[cut, :].astype(bf16)
        for e in range(local):
            piece = (dot(left, field[0][e]) + dot(right, field[1][e])).astype(bf16)
            for d in range(lat_count):
                part[i, d, e] = piece[d * 16 : (d + 1) * 16]
        if i == 0:
            pl.semaphore_wait(barrier, lat_count + chips - 1)
        for copy in first[i]:
            copy.start()

    for copy in load[5:]:
        copy.wait()
    size = bands * k_count
    spread = iota((k_count, size), 1) - bands * iota((k_count, size), 0)
    spread = ((spread >= 0) & (spread < bands)).astype(f32).astype(bf16)
    eye = iota((cells, cells), 0) == iota((cells, cells), 1)

    def column(row):
        return jnp.sum(jnp.where(eye, row, 0.0), axis=1, keepdims=True)

    column_of = [column(rv_ref[i : i + 1, :].astype(f32)) for i in range(3)]
    argument = two_pi * (
        kp_ref[0:1, :] * column_of[0] + kp_ref[1:2, :] * column_of[1] + kp_ref[2:3, :] * column_of[2]
    )
    inverse = 1.0 / column(rw_ref[...].astype(f32))
    p2[0] = dot((jnp.cos(argument) * inverse).astype(bf16), spread)
    p2[1] = dot((jnp.sin(argument) * inverse).astype(bf16), spread)

    row = iota((width, size), 0)
    lane = iota((width, size), 1) & (bands - 1)
    pick = iota((bands, width), 1)
    order = iota((bands, width), 0)
    minor = (row & (bands - 1)) == lane
    major = (row // bands) == lane
    take_major = ((pick // bands) == order).astype(f32).astype(bf16)
    take_minor = ((pick & (bands - 1)) == order).astype(f32).astype(bf16)
    keep = jnp.concatenate([mk_ref[...].astype(f32)] * bands, axis=0)
    for c in range(2):
        wide = dot((u_ref[c].astype(f32) * keep).astype(bf16), spread)
        u2[c] = dot(take_major, jnp.where(minor, wide, 0.0).astype(bf16))
    blocks = gs.shape[0] // 2
    lanes = gs.shape[2]

    def grow(e, carry):
        pr, pi = p2[0, pl.ds(e, 1), :], p2[1, pl.ds(e, 1), :]
        re = (pr * u2[0] - pi * u2[1]).astype(bf16)
        im = pr * u2[1] + pi * u2[0]
        minus = (-im).astype(bf16)
        im = im.astype(bf16)
        at = pl.ds(pl.multiple_of(e * 2 * bands, bands), bands)
        below = pl.ds(pl.multiple_of(e * 2 * bands + bands, bands), bands)
        for t in range(blocks):
            cut = slice(t * lanes, (t + 1) * lanes)
            gs[t, at, :] = re[:, cut]
            gs[blocks + t, at, :] = im[:, cut]
            gs[t, below, :] = minus[:, cut]
            gs[blocks + t, below, :] = re[:, cut]
        return carry

    lax.fori_loop(0, cells, grow, 0)

    tall = 2 * bands * span * q_count

    def lay(stage):
        if stage == 0:
            for q in range(q_count):
                keep = jnp.concatenate([mkq_ref[q].astype(f32)] * bands, axis=0)
                turn = []
                for c in range(2):
                    wide = dot((v_ref[c, q].astype(f32) * keep).astype(bf16), spread)
                    turn.append(dot(take_minor, jnp.where(major, wide, 0.0).astype(bf16)).astype(bf16))
                at = q * 2 * bands
                v2[0, at : at + bands, :], v2[0, at + bands : at + 2 * bands, :] = turn[0], -turn[1]
                v2[1, at : at + bands, :], v2[1, at + bands : at + 2 * bands, :] = turn[1], turn[0]
            return
        row = iota((tall, LANES), 0)
        at_k = ((row // (span * 16)) & (span // quad - 1)) * quad + ((row // (halves * q_count)) & (quad - 1))
        same = at_k == iota((tall, LANES), 1) // bands
        row = iota((tall, q_count * 2 * bands), 0)
        band = ((row // q_count) & (halves - 1)) * span + ((row // 16) & (span - 1))
        band = ((row & (q_count - 1)) * 2 + row // (tall // 2)) * bands + band
        repeat = (band == iota((tall, q_count * 2 * bands), 1)).astype(f32).astype(bf16)
        for o in range(k_count // span):
            for c in range(2):
                wide = dot(repeat, v2[c, :, o * LANES : (o + 1) * LANES])
                vb[o, :, c * LANES : (c + 1) * LANES] = jnp.where(same, wide, 0.0).astype(bf16)

    def over(source, i, target, send_sem, recv_sem):
        return pltpu.make_async_remote_copy(
            src_ref=gath.at[source, i],
            dst_ref=gath.at[source, i],
            send_sem=send_sem,
            recv_sem=recv_sem,
            device_id=(lat, target),
            device_id_type=MESH,
        )

    def outward(i, act):
        for down, some in ((True, [0]), (False, reversed(range(chips))), (True, range(1, chips))):
            for z in some:

                @pl.when((chip > z) if down else (chip < z))
                def _():
                    act(over(kpt, i, 2 * z + core, chip_send.at[i, z], chip_recv.at[i, chip]))

    def start(copy):
        copy.start()

    def sent(copy):
        copy.wait_send()

    third = []

    def pass_on(source, i, step):
        copy = over(source, i, pair, pair_send.at[i, step], pair_recv.at[i, step])
        copy.start()
        third.append((copy, step))

    def begin(near):
        for copy, step in third:
            if step in (0, chips - 1):
                copy.wait_recv()
        for t in range(2 * blocks):
            acc[t] = cell_sum(t, [2 * z + c for z in (chip, near) for c in range(2)], gath, gs)

    cut = span // 2
    for i in range(sets):
        for copy in first[i]:
            copy.wait_recv()
        for g in range(local // cut):
            rows = []
            for e in range(g * cut, (g + 1) * cut):
                total = part[i, lat, e].astype(f32)
                for step in range(1, lat_count):
                    total = total + recv[i, lat_peer(step), e].astype(f32)
                rows += [total[:8], total[8:]]
            for h in range(halves):
                tiles = exchange([r[:, h * LANES : (h + 1) * LANES] for r in rows], bands)
                for a in range(span):
                    turned[pl.ds(h * span + a, 8, stride=bands), :] = tiles[a]
            gath[kpt, i, g] = turned[...].astype(bf16)
        outward(i, start)
        pass_on(kpt, i, chips - 1)

    nearest = [apart(chip, chips, step) for step in range(chips - 1)]
    waits = sorted(
        ((i + min(step, 1) + 0.1 * step, step, i) for step in range(chips - 1) for i in range(sets))
    )
    ready = [n for n, (_, step, _) in enumerate(waits) if step == 0][-1] + 1
    stage = 0
    for n, (_, step, i) in enumerate(waits):
        if stage < 2 and n in (1, 3):
            lay(stage)
            stage += 1
        if n == ready:
            begin(nearest[0])
        source = nearest[step]
        over(2 * source + core, i, pair, chip_send.at[i, 0], chip_recv.at[i, source]).wait_recv()
        pass_on(2 * source + core, i, step)
    while stage < 2:
        lay(stage)
        stage += 1
    if ready >= len(waits):
        begin(nearest[0])
    straight = [2 * z + core for z in nearest[1:]]
    for t in range(2 * blocks):
        acc[t] += cell_sum(t, straight, gath, gs)
    for copy, step in third:
        if 0 < step < chips - 1:
            copy.wait_recv()
    for copies in first:
        for copy in copies:
            copy.wait_send()
    for copy, _ in third:
        copy.wait_send()
    for i in range(sets):
        outward(i, sent)


def couple_kernel(modes, q_count, bands, gath, gs, vb, acc, out_ref, rt, scr, sems):
    blocks = gs.shape[0] // 2
    span = LANES // bands
    near = gs.shape[2] // LANES
    k_count = near * blocks * span
    held = out_ref.shape[1]
    chips = gath.shape[0] // 2
    chip, core = lax.axis_index("kpt") // 2, lax.axis_index("kpt") % 2
    rest = [2 * apart(chip, chips, step) + 1 - core for step in range(1, chips - 1)]

    def total(t):
        return tuple(
            (acc[c * blocks + t] + cell_sum(c * blocks + t, rest, gath, gs)).astype(bf16) for c in range(2)
        )

    def leave(t):
        copies = []
        for c in range(2):
            rows = pl.ds(c * k_count + t * span, span)
            copies.append(pltpu.make_async_copy(scr.at[rows, :held], out_ref.at[rows], sems.at[t, c]))
        return copies

    def step(t, field):
        ahead = total(t + 1) if t + 1 < blocks else None
        finish(t, field, modes, q_count, bands, range(modes // 8), modes % 8, gs, vb, rt, scr, leave)
        return ahead

    field = total(0)
    for t in range(blocks):
        field = step(t, field)
    for t in range(near * blocks):
        for copy in leave(t):
            copy.wait()


def per_device(
    lat_count,
    kpt_count,
    coarse,
    rp_vectors,
    rp_weights,
    re_vectors,
    re_weights,
    q_points,
    k_points,
    modes_rot,
    u_k,
    u_kq,
    mask_k,
    mask_kq,
):
    q_count = q_points.shape[0]
    k_count = k_points.shape[0]
    bands = u_k.shape[2]
    width = bands * bands
    local = coarse.shape[2]
    mode_count = coarse.shape[3] // width
    modes = mode_count // lat_count
    cells = re_vectors.shape[0]
    span = LANES // bands
    qn = modes // 8 * 8 * q_count + up(modes % 8 * q_count, 8)
    sets = qn // 8
    groups = local // (span // 2)
    octets = -(-modes // span)
    chips = kpt_count // 2
    lanes = 2 * LANES
    blocks = bands * k_count // lanes
    assert chips > 2 and coarse.shape[1] == 1 and local % (span // 2) == 0 and bands & (bands - 1) == 0

    uk = jnp.transpose(u_k, (0, 2, 3, 1)).reshape(2, width, k_count)
    ukq = jnp.transpose(u_kq, (0, 1, 3, 4, 2)).reshape(2, q_count, width, k_count)
    keep_k = jnp.transpose(mask_k)
    keep_kq = jnp.transpose(mask_kq, (0, 2, 1))

    anywhere = pl.BlockSpec(memory_space=pltpu.HBM)
    vmem = pl.BlockSpec(memory_space=pltpu.VMEM)
    dma = pltpu.SemaphoreType.DMA
    tall = span * q_count * 2 * bands
    inputs = (
        q_points,
        rp_vectors,
        rp_weights.reshape(1, 1),
        coarse,
        modes_rot,
        jnp.transpose(re_vectors),
        re_weights.reshape(1, cells),
        jnp.transpose(k_points),
        uk,
        ukq,
        keep_k,
        keep_kq,
    )
    count = modes * (width // LANES)
    held = count * q_count
    shapes = [
        ((kpt_count, sets, groups, 8 * bands, LANES), bf16),
        ((2 * blocks, 2 * cells * bands, lanes), bf16),
        ((k_count // span, tall, 2 * LANES), bf16),
        ((2 * blocks, qn * bands, lanes), f32),
    ]
    kept = sum(4 * math.prod(shape) for shape, _ in shapes[3:]) + sum(2 * math.prod(shape) for shape, _ in shapes[:3])
    parts = pl.pallas_call(
        functools.partial(gather_kernel, lat_count, kpt_count, modes),
        in_specs=[anywhere] * len(inputs),
        out_specs=[vmem] * len(shapes),
        out_shape=[pltpu.VMEM(shape, dtype) for shape, dtype in shapes],
        scratch_shapes=[pltpu.VMEM(x.shape, x.dtype) for x in inputs]
        + [
            pltpu.VMEM((2 * local * mode_count * (width // LANES), LANES), f32),
            pltpu.VMEM((lat_count * 2 * qn, mode_count), f32),
            pltpu.VMEM((lat_count * 2 * qn, mode_count), f32),
            pltpu.VMEM((sets, lat_count, local, 16, width), bf16),
            pltpu.VMEM((sets, lat_count, local, 16, width), bf16),
            pltpu.VMEM((8 * bands, LANES), f32),
            pltpu.VMEM((2, cells, bands * k_count), f32),
            pltpu.VMEM((2, bands, bands * k_count), f32),
            pltpu.VMEM((2, q_count * 2 * bands, bands * k_count), bf16),
            dma((len(inputs),)),
            dma((sets, lat_count)),
            dma((sets, lat_count)),
            dma((sets, chips)),
            dma((sets, chips)),
            dma((sets, chips)),
            dma((sets, chips)),
        ],
        compiler_params=pltpu.CompilerParams(
            collective_id=0, has_side_effects=True, vmem_limit_bytes=63 * 1024 * 1024 - kept
        ),
    )(*inputs)
    result = jax.ShapeDtypeStruct((2 * k_count, held, LANES), bf16)
    out = pl.pallas_call(
        functools.partial(couple_kernel, modes, q_count, bands),
        in_specs=[vmem] * len(parts),
        out_specs=anywhere,
        out_shape=result,
        scratch_shapes=[
            pltpu.VMEM((lanes // LANES, sets, 2 * LANES, LANES), bf16),
            pltpu.VMEM((2 * k_count, up(held, 16), LANES), bf16),
            dma((k_count // span, 2)),
        ],
        compiler_params=pltpu.CompilerParams(vmem_limit_bytes=40 * 1024 * 1024),
    )(*parts)
    out = out.reshape(2, k_count, count, q_count, LANES)
    return jnp.transpose(out, (0, 1, 3, 2, 4)).reshape(2, k_count, q_count, modes * width)


def solution(mesh):
    placed = (
        P(None, "lat", "kpt", None),
        P("lat", None),
        P("lat"),
        P(),
        P(),
        P(),
        P("kpt", None),
        P(),
        P(None, "kpt", None, None),
        P(None, None, "kpt", None, None),
        P("kpt", None),
        P(None, "kpt", None),
    )
    return jax.shard_map(
        functools.partial(per_device, mesh.shape["lat"], mesh.shape["kpt"]),
        mesh=mesh,
        in_specs=placed,
        out_specs=P(None, "kpt", None, "lat"),
        check_vma=False,
    )
```

```python
import functools
import math

import jax
import jax.numpy as jnp
from jax import lax
from jax.experimental import pallas as pl
from jax.experimental.pallas import tpu as pltpu
from jax.sharding import PartitionSpec as P

two_pi = 6.283185307179586
f32 = jnp.float32
bf16 = jnp.bfloat16
i32 = jnp.int32
MESH = pl.DeviceIdType.MESH
LANES = 128


def up(value, step):
    return -(-value // step) * step


def iota(shape, axis):
    return lax.broadcasted_iota(i32, shape, axis)


def dot(a, b):
    return jnp.dot(a, b, preferred_element_type=f32)


def exchange(tiles, unit, axis=1):
    span = len(tiles)
    shape = next(t for t in tiles if t is not None).shape
    place = iota(shape, axis)
    skew = [t if i == 0 or t is None else pltpu.roll(t, i * unit, axis) for i, t in enumerate(tiles)]
    tiles = [skew[-i % span] for i in range(span)]
    bit = 1
    while bit < span:
        odd = (place & (unit * bit)) != 0
        turned = []
        for i in range(span):
            a, b = tiles[i], tiles[(i - bit) % span]
            turned.append(b if a is None else a if b is None else jnp.where(odd, b, a))
        tiles = turned
        bit *= 2
    return [t if i == 0 else pltpu.roll(t, shape[axis] - i * unit, axis) for i, t in enumerate(tiles)]


def apart(chip, chips, step):
    found = 0
    for z in range(chips):
        others = sorted((o for o in range(chips) if o != z), key=lambda o: abs(o - z))
        found = found + jnp.where(chip == z, others[step], 0)
    return found


def cell_sum(t, some, gath, gs):
    _, sets, groups = gath.shape[:3]
    deep = groups * LANES
    left = jnp.concatenate(
        [
            jnp.concatenate([gath[j, i, g] for j in some for g in range(groups)], axis=1)
            for i in range(sets)
        ],
        axis=0,
    )
    right = [gs[t, pl.ds(pl.multiple_of(j * deep, deep), deep), :] for j in some]
    return dot(left, jnp.concatenate(right, axis=0))


def finish(t, field, modes, q_count, bands, octets, rest, gs, vb, rt, scr, leave):
    blocks = gs.shape[0] // 2
    near = gs.shape[2] // LANES
    span = LANES // bands
    halves = bands * bands // LANES
    quad = 16 // (halves * q_count)
    many = span // quad
    k_count = near * blocks * span
    last = modes // 8 * q_count
    sets = [j * q_count + q for j in octets for q in range(q_count)] + ([last] if rest else [])
    for c in range(2):
        for o in range(near):
            for n in range(len(sets)):
                tiles = []
                for i in range(8):
                    at = (n * 8 + i) * bands
                    tiles.append(field[c][at : at + bands, o * LANES : (o + 1) * LANES])
                for i, tile in enumerate(exchange(tiles, bands)):
                    at = (c * span + i) * bands
                    rt[o, n, at : at + bands, :] = tile
    turn = iota((16, LANES), 0) & (q_count - 1)

    def choose(tiles):
        tile = tiles[0]
        for q in range(1, q_count):
            tile = jnp.where(turn == q, tiles[q], tile)
        return tile

    for o in range(near):
        right = jnp.concatenate([rt[o, n] for n in range(len(sets))], axis=1)
        done = dot(vb[t * near + o], right)
        for c in range(2):
            for g in range(many):
                base = (c * many + g) * span * 16

                def tile(n, i):
                    at = base + i * 16
                    return done[at : at + 16, n * LANES : (n + 1) * LANES].astype(bf16)

                found = []
                for j in range(len(octets)):
                    found += exchange(
                        [choose([tile(j * q_count + q, i) for q in range(q_count)]) for i in range(span)], bands
                    )
                if rest:
                    tiles = exchange([tile(len(sets) - 1, i) for i in range(span)], bands)
                    found += [choose([tiles[q * rest + i] for q in range(q_count)]) for i in range(rest)]
                for m in range(0, len(found), quad):
                    tiles = (found[m : m + quad] + [None] * quad)[:quad]
                    tiles = exchange(tiles, halves * q_count, 0)
                    at = m * halves * q_count
                    tall = min(quad, len(found) - m) * halves * q_count
                    for i in range(quad):
                        k = (t * near + o) * span + g * quad + i
                        scr[c * k_count + k, at : at + tall, :] = tiles[i][:tall]
        for copy in leave(t * near + o):
            copy.start()


def gather_kernel(
    lat_count,
    kpt_count,
    modes,
    qp_hbm,
    rpv_hbm,
    rpw_hbm,
    x_hbm,
    rot_hbm,
    rv_hbm,
    rw_hbm,
    kp_hbm,
    u_hbm,
    v_hbm,
    mk_hbm,
    mkq_hbm,
    gath,
    gs,
    vb,
    acc,
    qp,
    rpv,
    rpw,
    x_ref,
    rot_ref,
    rv_ref,
    rw_ref,
    kp_ref,
    u_ref,
    v_ref,
    mk_ref,
    mkq_ref,
    xs,
    wre,
    wim,
    part,
    recv,
    turned,
    p2,
    u2,
    v2,
    loads,
    lat_send,
    lat_recv,
    chip_send,
    chip_recv,
    pair_send,
    pair_recv,
):
    given = (qp_hbm, rpv_hbm, rpw_hbm, x_hbm, rot_hbm, rv_hbm, rw_hbm, kp_hbm, u_hbm, v_hbm, mk_hbm, mkq_hbm)
    held = (qp, rpv, rpw, x_ref, rot_ref, rv_ref, rw_ref, kp_ref, u_ref, v_ref, mk_ref, mkq_ref)
    load = []
    for i in range(len(given)):
        load.append(pltpu.make_async_copy(given[i], held[i], loads.at[i]))
    for i in (3, 4, 0, 1, 2, *range(5, len(given))):
        load[i].start()
    lat = lax.axis_index("lat")
    kpt = lax.axis_index("kpt")
    chips = kpt_count // 2
    chip = kpt // 2
    core = kpt - 2 * chip
    pair = 2 * chip + 1 - core

    def lat_peer(step):
        return lax.rem(lat + step, lat_count)

    def chip_peer(step):
        return lax.rem(chip + step, chips)

    barrier = pltpu.get_barrier_semaphore()
    for step in range(1, lat_count):
        pl.semaphore_signal(barrier, inc=1, device_id=(lat_peer(step), kpt), device_id_type=MESH)
    for step in range(1, chips):
        pl.semaphore_signal(barrier, inc=1, device_id=(lat, 2 * chip_peer(step) + core), device_id_type=MESH)
    pl.semaphore_signal(barrier, inc=1, device_id=(lat, pair), device_id_type=MESH)

    q_count = rot_ref.shape[1]
    mode_count = rot_ref.shape[2]
    local = x_ref.shape[2]
    bands = mk_ref.shape[0]
    k_count = mk_ref.shape[1]
    width = bands * bands
    halves = width // LANES
    cells = rv_ref.shape[1]
    sets = part.shape[0]
    qn = sets * 8
    span = LANES // bands
    quad = 16 // (halves * q_count)

    for copy in load[:5]:
        copy.wait()
    if q_count * modes != qn:
        wre[...] = jnp.zeros_like(wre)
        wim[...] = jnp.zeros_like(wim)
    for q in range(q_count):
        term = qp[q : q + 1, :] * rpv[...].astype(f32)
        argument = two_pi * (term[:, 0:1] + term[:, 1:2] + term[:, 2:3])
        argument = jnp.broadcast_to(argument, (1, mode_count))
        inverse = 1.0 / jnp.broadcast_to(rpw[...].astype(f32).reshape(1, 1), (1, mode_count))
        pr = (jnp.cos(argument) * inverse).astype(bf16).astype(f32)
        pi = (jnp.sin(argument) * inverse).astype(bf16).astype(f32)
        mr = rot_ref[0, q].astype(f32).T
        mi = rot_ref[1, q].astype(f32).T
        wr = pr * mr - pi * mi
        wi = pr * mi + pi * mr
        for d in range(lat_count):
            rest = modes % 8
            for n in range(0, modes, 8):
                take = min(8, modes - n)
                rows = slice(d * modes + n, d * modes + n + take)
                at = ((n // 8 * q_count + q) * lat_count + d) * 16
                if take == rest:
                    at = (n // 8 * q_count * lat_count + d) * 16 + q * rest
                wre[at : at + take, :] = wr[rows]
                wim[at : at + take, :] = -wi[rows]
                wre[at + 8 : at + 8 + take, :] = wi[rows]
                wim[at + 8 : at + 8 + take, :] = wr[rows]

    for c in range(2):
        x = x_ref[c, 0].astype(f32)
        for m in range(mode_count):
            for h in range(halves):
                at = (h * mode_count + m) * 2 * local + c * local
                lane = m * width + h * LANES
                xs[at : at + local, :] = x[:, lane : lane + LANES]

    def rows_of(c, e):
        return jnp.concatenate(
            [
                xs[pl.ds(h * mode_count * 2 * local + c * local + e, mode_count, stride=2 * local), :]
                for h in range(halves)
            ],
            axis=1,
        ).astype(bf16)

    first = [
        [
            pltpu.make_async_remote_copy(
                src_ref=part.at[i, lat_peer(step)],
                dst_ref=recv.at[i, lat],
                send_sem=lat_send.at[i, step],
                recv_sem=lat_recv.at[i, step],
                device_id=(lat_peer(step), kpt),
                device_id_type=MESH,
            )
            for step in range(1, lat_count)
        ]
        for i in range(sets)
    ]
    field = [[rows_of(c, e) for e in range(local)] for c in range(2)]
    for i in range(sets):
        cut = slice(i * lat_count * 16, (i + 1) * lat_count * 16)
        left, right = wre[cut, :].astype(bf16), wim[cut, :].astype(bf16)
        for e in range(local):
            piece = (dot(left, field[0][e]) + dot(right, field[1][e])).astype(bf16)
            for d in range(lat_count):
                part[i, d, e] = piece[d * 16 : (d + 1) * 16]
        if i == 0:
            pl.semaphore_wait(barrier, lat_count + chips - 1)
        for copy in first[i]:
            copy.start()

    for copy in load[5:]:
        copy.wait()
    size = bands * k_count
    spread = iota((k_count, size), 1) - bands * iota((k_count, size), 0)
    spread = ((spread >= 0) & (spread < bands)).astype(f32).astype(bf16)
    eye = iota((cells, cells), 0) == iota((cells, cells), 1)

    def column(row):
        return jnp.sum(jnp.where(eye, row, 0.0), axis=1, keepdims=True)

    column_of = [column(rv_ref[i : i + 1, :].astype(f32)) for i in range(3)]
    argument = two_pi * (
        kp_ref[0:1, :] * column_of[0] + kp_ref[1:2, :] * column_of[1] + kp_ref[2:3, :] * column_of[2]
    )
    inverse = 1.0 / column(rw_ref[...].astype(f32))
    p2[0] = dot((jnp.cos(argument) * inverse).astype(bf16), spread)
    p2[1] = dot((jnp.sin(argument) * inverse).astype(bf16), spread)

    row = iota((width, size), 0)
    lane = iota((width, size), 1) & (bands - 1)
    pick = iota((bands, width), 1)
    order = iota((bands, width), 0)
    minor = (row & (bands - 1)) == lane
    major = (row // bands) == lane
    take_major = ((pick // bands) == order).astype(f32).astype(bf16)
    take_minor = ((pick & (bands - 1)) == order).astype(f32).astype(bf16)
    keep = jnp.concatenate([mk_ref[...].astype(f32)] * bands, axis=0)
    for c in range(2):
        wide = dot((u_ref[c].astype(f32) * keep).astype(bf16), spread)
        u2[c] = dot(take_major, jnp.where(minor, wide, 0.0).astype(bf16))
    blocks = gs.shape[0] // 2
    lanes = gs.shape[2]

    def grow(e, carry):
        pr, pi = p2[0, pl.ds(e, 1), :], p2[1, pl.ds(e, 1), :]
        re = (pr * u2[0] - pi * u2[1]).astype(bf16)
        im = pr * u2[1] + pi * u2[0]
        minus = (-im).astype(bf16)
        im = im.astype(bf16)
        at = pl.ds(pl.multiple_of(e * 2 * bands, bands), bands)
        below = pl.ds(pl.multiple_of(e * 2 * bands + bands, bands), bands)
        for t in range(blocks):
            cut = slice(t * lanes, (t + 1) * lanes)
            gs[t, at, :] = re[:, cut]
            gs[blocks + t, at, :] = im[:, cut]
            gs[t, below, :] = minus[:, cut]
            gs[blocks + t, below, :] = re[:, cut]
        return carry

    lax.fori_loop(0, cells, grow, 0)

    tall = 2 * bands * span * q_count

    def lay(stage):
        if stage == 0:
            for q in range(q_count):
                keep = jnp.concatenate([mkq_ref[q].astype(f32)] * bands, axis=0)
                turn = []
                for c in range(2):
                    wide = dot((v_ref[c, q].astype(f32) * keep).astype(bf16), spread)
                    turn.append(dot(take_minor, jnp.where(major, wide, 0.0).astype(bf16)).astype(bf16))
                at = q * 2 * bands
                v2[0, at : at + bands, :], v2[0, at + bands : at + 2 * bands, :] = turn[0], -turn[1]
                v2[1, at : at + bands, :], v2[1, at + bands : at + 2 * bands, :] = turn[1], turn[0]
            return
        row = iota((tall, LANES), 0)
        at_k = ((row // (span * 16)) & (span // quad - 1)) * quad + ((row // (halves * q_count)) & (quad - 1))
        same = at_k == iota((tall, LANES), 1) // bands
        row = iota((tall, q_count * 2 * bands), 0)
        band = ((row // q_count) & (halves - 1)) * span + ((row // 16) & (span - 1))
        band = ((row & (q_count - 1)) * 2 + row // (tall // 2)) * bands + band
        repeat = (band == iota((tall, q_count * 2 * bands), 1)).astype(f32).astype(bf16)
        for o in range(k_count // span):
            for c in range(2):
                wide = dot(repeat, v2[c, :, o * LANES : (o + 1) * LANES])
                vb[o, :, c * LANES : (c + 1) * LANES] = jnp.where(same, wide, 0.0).astype(bf16)

    def over(source, i, target, send_sem, recv_sem):
        return pltpu.make_async_remote_copy(
            src_ref=gath.at[source, i],
            dst_ref=gath.at[source, i],
            send_sem=send_sem,
            recv_sem=recv_sem,
            device_id=(lat, target),
            device_id_type=MESH,
        )

    def outward(i, act):
        for down, some in ((True, [0]), (False, reversed(range(chips))), (True, range(1, chips))):
            for z in some:

                @pl.when((chip > z) if down else (chip < z))
                def _():
                    act(over(kpt, i, 2 * z + core, chip_send.at[i, z], chip_recv.at[i, chip]))

    def start(copy):
        copy.start()

    def sent(copy):
        copy.wait_send()

    third = []

    def pass_on(source, i, step):
        copy = over(source, i, pair, pair_send.at[i, step], pair_recv.at[i, step])
        copy.start()
        third.append((copy, step))

    def begin(near):
        for copy, step in third:
            if step in (0, chips - 1):
                copy.wait_recv()
        for t in range(2 * blocks):
            acc[t] = cell_sum(t, [2 * z + c for z in (chip, near) for c in range(2)], gath, gs)

    cut = span // 2
    for i in range(sets):
        for copy in first[i]:
            copy.wait_recv()
        for g in range(local // cut):
            rows = []
            for e in range(g * cut, (g + 1) * cut):
                total = part[i, lat, e].astype(f32)
                for step in range(1, lat_count):
                    total = total + recv[i, lat_peer(step), e].astype(f32)
                rows += [total[:8], total[8:]]
            for h in range(halves):
                tiles = exchange([r[:, h * LANES : (h + 1) * LANES] for r in rows], bands)
                for a in range(span):
                    turned[pl.ds(h * span + a, 8, stride=bands), :] = tiles[a]
            gath[kpt, i, g] = turned[...].astype(bf16)
        outward(i, start)
        pass_on(kpt, i, chips - 1)

    nearest = [apart(chip, chips, step) for step in range(chips - 1)]
    waits = sorted(
        ((i + min(step, 1) + 0.1 * step, step, i) for step in range(chips - 1) for i in range(sets))
    )
    ready = [n for n, (_, step, _) in enumerate(waits) if step == 0][-1] + 1
    stage = 0
    for n, (_, step, i) in enumerate(waits):
        if stage < 2 and n in (1, 3):
            lay(stage)
            stage += 1
        if n == ready:
            begin(nearest[0])
        source = nearest[step]
        over(2 * source + core, i, pair, chip_send.at[i, 0], chip_recv.at[i, source]).wait_recv()
        pass_on(2 * source + core, i, step)
    while stage < 2:
        lay(stage)
        stage += 1
    if ready >= len(waits):
        begin(nearest[0])
    straight = [2 * z + core for z in nearest[1:]]
    for t in range(2 * blocks):
        acc[t] += cell_sum(t, straight, gath, gs)
    for copy, step in third:
        if 0 < step < chips - 1:
            copy.wait_recv()
    for copies in first:
        for copy in copies:
            copy.wait_send()
    for copy, _ in third:
        copy.wait_send()
    for i in range(sets):
        outward(i, sent)


def couple_kernel(modes, q_count, bands, gath, gs, vb, acc, out_ref, rt, scr, sems):
    blocks = gs.shape[0] // 2
    span = LANES // bands
    near = gs.shape[2] // LANES
    k_count = near * blocks * span
    held = out_ref.shape[1]
    chips = gath.shape[0] // 2
    chip, core = lax.axis_index("kpt") // 2, lax.axis_index("kpt") % 2
    rest = [2 * apart(chip, chips, step) + 1 - core for step in range(1, chips - 1)]

    def total(t):
        return tuple(
            (acc[c * blocks + t] + cell_sum(c * blocks + t, rest, gath, gs)).astype(bf16) for c in range(2)
        )

    def leave(t):
        copies = []
        for c in range(2):
            rows = pl.ds(c * k_count + t * span, span)
            copies.append(pltpu.make_async_copy(scr.at[rows, :held], out_ref.at[rows], sems.at[t, c]))
        return copies

    def step(t, field):
        ahead = total(t + 1) if t + 1 < blocks else None
        finish(t, field, modes, q_count, bands, range(modes // 8), modes % 8, gs, vb, rt, scr, leave)
        return ahead

    field = total(0)
    for t in range(blocks):
        field = step(t, field)
    for t in range(near * blocks):
        for copy in leave(t):
            copy.wait()


def per_device(
    lat_count,
    kpt_count,
    coarse,
    rp_vectors,
    rp_weights,
    re_vectors,
    re_weights,
    q_points,
    k_points,
    modes_rot,
    u_k,
    u_kq,
    mask_k,
    mask_kq,
):
    q_count = q_points.shape[0]
    k_count = k_points.shape[0]
    bands = u_k.shape[2]
    width = bands * bands
    local = coarse.shape[2]
    mode_count = coarse.shape[3] // width
    modes = mode_count // lat_count
    cells = re_vectors.shape[0]
    span = LANES // bands
    qn = modes // 8 * 8 * q_count + up(modes % 8 * q_count, 8)
    sets = qn // 8
    groups = local // (span // 2)
    octets = -(-modes // span)
    chips = kpt_count // 2
    lanes = 2 * LANES
    blocks = bands * k_count // lanes
    assert chips > 2 and coarse.shape[1] == 1 and local % (span // 2) == 0 and bands & (bands - 1) == 0

    uk = jnp.transpose(u_k, (0, 2, 3, 1)).reshape(2, width, k_count)
    ukq = jnp.transpose(u_kq, (0, 1, 3, 4, 2)).reshape(2, q_count, width, k_count)
    keep_k = jnp.transpose(mask_k)
    keep_kq = jnp.transpose(mask_kq, (0, 2, 1))

    anywhere = pl.BlockSpec(memory_space=pltpu.HBM)
    vmem = pl.BlockSpec(memory_space=pltpu.VMEM)
    dma = pltpu.SemaphoreType.DMA
    tall = span * q_count * 2 * bands
    inputs = (
        q_points,
        rp_vectors,
        rp_weights,
        coarse,
        modes_rot,
        jnp.transpose(re_vectors),
        re_weights.reshape(1, cells),
        jnp.transpose(k_points),
        uk,
        ukq,
        keep_k,
        keep_kq,
    )
    count = modes * (width // LANES)
    held = count * q_count
    shapes = [
        ((kpt_count, sets, groups, 8 * bands, LANES), bf16),
        ((2 * blocks, 2 * cells * bands, lanes), bf16),
        ((k_count // span, tall, 2 * LANES), bf16),
        ((2 * blocks, qn * bands, lanes), f32),
    ]
    kept = sum(4 * math.prod(shape) for shape, _ in shapes[3:]) + sum(2 * math.prod(shape) for shape, _ in shapes[:3])
    parts = pl.pallas_call(
        functools.partial(gather_kernel, lat_count, kpt_count, modes),
        in_specs=[anywhere] * len(inputs),
        out_specs=[vmem] * len(shapes),
        out_shape=[pltpu.VMEM(shape, dtype) for shape, dtype in shapes],
        scratch_shapes=[pltpu.VMEM(x.shape, x.dtype) for x in inputs]
        + [
            pltpu.VMEM((2 * local * mode_count * (width // LANES), LANES), f32),
            pltpu.VMEM((lat_count * 2 * qn, mode_count), f32),
            pltpu.VMEM((lat_count * 2 * qn, mode_count), f32),
            pltpu.VMEM((sets, lat_count, local, 16, width), bf16),
            pltpu.VMEM((sets, lat_count, local, 16, width), bf16),
            pltpu.VMEM((8 * bands, LANES), f32),
            pltpu.VMEM((2, cells, bands * k_count), f32),
            pltpu.VMEM((2, bands, bands * k_count), f32),
            pltpu.VMEM((2, q_count * 2 * bands, bands * k_count), bf16),
            dma((len(inputs),)),
            dma((sets, lat_count)),
            dma((sets, lat_count)),
            dma((sets, chips)),
            dma((sets, chips)),
            dma((sets, chips)),
            dma((sets, chips)),
        ],
        compiler_params=pltpu.CompilerParams(
            collective_id=0, has_side_effects=True, vmem_limit_bytes=63 * 1024 * 1024 - kept
        ),
    )(*inputs)
    result = jax.ShapeDtypeStruct((2 * k_count, held, LANES), bf16)
    out = pl.pallas_call(
        functools.partial(couple_kernel, modes, q_count, bands),
        in_specs=[vmem] * len(parts),
        out_specs=anywhere,
        out_shape=result,
        scratch_shapes=[
            pltpu.VMEM((lanes // LANES, sets, 2 * LANES, LANES), bf16),
            pltpu.VMEM((2 * k_count, up(held, 16), LANES), bf16),
            dma((k_count // span, 2)),
        ],
        compiler_params=pltpu.CompilerParams(vmem_limit_bytes=40 * 1024 * 1024),
    )(*parts)
    out = out.reshape(2, k_count, count, q_count, LANES)
    return jnp.transpose(out, (0, 1, 3, 2, 4)).reshape(2, k_count, q_count, modes * width)


def solution(mesh):
    placed = (
        P(None, "lat", "kpt", None),
        P("lat", None),
        P("lat"),
        P(),
        P(),
        P(),
        P("kpt", None),
        P(),
        P(None, "kpt", None, None),
        P(None, None, "kpt", None, None),
        P("kpt", None),
        P(None, "kpt", None),
    )
    return jax.shard_map(
        functools.partial(per_device, mesh.shape["lat"], mesh.shape["kpt"]),
        mesh=mesh,
        in_specs=placed,
        out_specs=P(None, "kpt", None, "lat"),
        check_vma=False,
    )
```
